256 devices in a mesh: blk: 32 (over z, y_lo, core), chan: 8 (over y_hi, x).
Axes of the slice: x: 4, y: 4 (y_hi: 2, y_lo: 2; y = y_hi * 2 + y_lo), z: 8, core: 2. Of those that a mesh axis runs over, the one named last changes fastest.
Arguments:
- spec_in: bfloat16 [256, 2, 512, 128], P('chan', None, 'blk'), may hold values from -6 to 6
- weight: bfloat16 [128, 2, 256, 256], P('blk', None, 'chan'), may hold values from -0.5 to 0.5
- pattern: int32 [128, 4, 4], P('blk'), may hold values 0 or 1
- cotangent: bfloat16 [256, 2, 512, 128], P('chan', None, 'blk'), may hold values from -6 to 6
Outputs:
- spec_out: bfloat16 [256, 2, 512, 128], P('chan', None, 'blk')
- grad_in: bfloat16 [256, 2, 512, 128], P('chan', None, 'blk')
- grad_weight: float32 [128, 2, 256, 256], P('blk', None, 'chan')
The draws below stay inside these ranges and needn't reach their ends.
All inputs are finite; a program needn't handle non-finite values. No bound on the sum of `pattern` on one device may be relied on, other than what follows from the above.
Results may differ from the reference program's by a relative error of at most 0.001.
Values may be sent and summed in bfloat16 or wider, within the bound.
A program may use at most 128 MiB of HBM per device.

```python
import jax
import jax.numpy as jnp
from jax import lax

C = 256
BLOCK = 64
NB = 4
SAMPLES = 512
MODES = 128


def with_ends(entries, own_key, least, largest):
    longest = entries.shape.index(max(entries.shape))
    spots = []
    for shift in (0, 1):
        where = [jax.random.randint(jax.random.fold_in(own_key, axis), (), 0, length) for axis, length in enumerate(entries.shape)]
        where[longest] = (where[longest] + shift) % entries.shape[longest]
        spots.append(tuple(where))
    return entries.at[spots[0]].set(least).at[spots[1]].set(largest)


def spiked(result, own_key, source, target, parts, factor):
    owner, partner = [(jnp.arange(result.shape[dim]) // (result.shape[dim] // parts)).reshape([-1 if axis == dim else 1 for axis in range(result.ndim)]) for dim in (source, target)]
    chosen = jax.random.permutation(own_key, parts)[partner]
    strong = (owner == chosen) | (owner == (partner + parts // 2) % parts)
    return jnp.where(strong, factor * result, result)


def steps_of(rng, shape, shards, least, largest):
    gain = 1.0
    for axis_at, shards_of in shards:
        draws = jax.random.uniform(jax.random.fold_in(jax.random.fold_in(rng, 6), axis_at), (shards_of,), jnp.float32, least / len(shards), largest / len(shards))
        gain = gain * jnp.repeat(jnp.exp(draws), shape[axis_at] // shards_of).reshape((-1,) + (1,) * (len(shape) - 1 - axis_at))
    return gain


def heavy_noise(stream_key, shape, width, bound, cuts, heavy, held_as=jnp.bfloat16):
    entries = width * jax.random.normal(stream_key, shape, jnp.float32)
    if cuts:
        entries = entries * steps_of(stream_key, shape, cuts, -0.22, 0.18)
    return jnp.clip(spiked(entries, jax.random.fold_in(stream_key, 3), *heavy), -bound, bound).astype(held_as)


def setup_inputs(seed: int = 0) -> dict:
    seeds = jax.random.split(jax.random.key(seed), 5)
    spec_in = heavy_noise(seeds[0], (C, 2, SAMPLES, MODES), 1.0, 6.0, ((0, 8), (2, 32)), (2, 3, 32, 2.75))
    weight = heavy_noise(seeds[1], (MODES, 2, C, C), C ** -0.5, 0.5, ((0, 32), (2, 8)), (2, 3, 8, 2.0))
    pattern = with_ends((jax.random.randint(seeds[2], (MODES, NB, NB), 0, 2) < 1).astype(jnp.int32), jax.random.fold_in(seeds[2], 1), 0, 1)
    cotangent = heavy_noise(seeds[3], (C, 2, SAMPLES, MODES), 1.0, 6.0, ((0, 8), (2, 32)), (2, 3, 32, 2.75))
    return {"spec_in": spec_in, "weight": weight, "pattern": pattern, "cotangent": cotangent}


def expand_mask(pattern, block_size):
    rows = jnp.repeat(pattern.astype(jnp.float32), block_size, axis=1)
    return jnp.repeat(rows, block_size, axis=2)


def product(form, left, right):
    return jnp.einsum(form, left, right, precision=lax.Precision.HIGHEST)


def reference(spec_in, weight, pattern, cotangent):
    block_mask = expand_mask(pattern, BLOCK)
    masked = weight.astype(jnp.float32) * block_mask[:, None]
    inputs = spec_in.astype(jnp.float32)
    grads = cotangent.astype(jnp.float32)
    w_real = masked[:, 0]
    w_imag = masked[:, 1]

    form = "ism,mio->osm"
    out_real = product(form, inputs[:, 0], w_real) - product(form, inputs[:, 1], w_imag)
    out_imag = product(form, inputs[:, 0], w_imag) + product(form, inputs[:, 1], w_real)
    spec_out = jnp.stack([out_real, out_imag], axis=1).astype(jnp.bfloat16)

    back = "osm,mio->ism"
    dx_real = product(back, grads[:, 0], w_real) + product(back, grads[:, 1], w_imag)
    dx_imag = product(back, grads[:, 1], w_real) - product(back, grads[:, 0], w_imag)
    grad_in = jnp.stack([dx_real, dx_imag], axis=1).astype(jnp.bfloat16)

    outer = "ism,osm->mio"
    dw_real = product(outer, inputs[:, 0], grads[:, 0]) + product(outer, inputs[:, 1], grads[:, 1])
    dw_imag = product(outer, inputs[:, 0], grads[:, 1]) - product(outer, inputs[:, 1], grads[:, 0])
    grad_weight = jnp.stack([dw_real * block_mask, dw_imag * block_mask], axis=1)
    return spec_out, grad_in, grad_weight
```

```python
import jax
import jax.numpy as jnp
from jax import lax
from jax.experimental import pallas as pl
from jax.experimental.pallas import tpu as pltpu
from jax.sharding import PartitionSpec as P

F32 = jnp.float32
BF16 = jnp.bfloat16
MESH = pl.DeviceIdType.MESH

NZ, NYL, NC, NYH, NX = 8, 2, 2, 2, 4
NJ = NZ * NYL
NCH = NYH * NX
NCHIP = NJ * NCH
CH = 32
S = 16
C = 256


def kernel(x_ref, w_ref, pat_ref, g_ref, out_ref, gin_ref, gw_ref,
           xf, b32, sbuf, xm, wmask, wrecv, wb, ebuf, ybuf, rbuf, gall, gwbuf, gwr,
           x_send, x_recv, x_loc, w_send, w_recv, y_send, y_recv, y_loc, d_send, d_recv):
    blk = lax.axis_index("blk")
    c = lax.axis_index("chan")
    core = blk % NC
    j = blk // NC
    z = j // NYL
    y = (c // NX) * NYL + j % NYL
    x = c % NX

    def at(t):
        tz = (z + t % NZ) % NZ
        ty = (y + (t // NZ) % (NYL * NYH)) % (NYL * NYH)
        tx = (x + t // (NZ * NYL * NYH)) % NX
        return tz * NYL + ty % NYL, (ty // NYL) * NX + tx

    barrier = pltpu.get_barrier_semaphore()

    def greet(t, carry):
        tj, tc = at(t)
        pl.semaphore_signal(barrier, inc=1, device_id={"blk": tj * NC + core, "chan": tc}, device_id_type=MESH)
        return carry

    lax.fori_loop(1, NCHIP, greet, 0)

    def greet_other(k, carry):
        pl.semaphore_signal(barrier, inc=1, device_id={"blk": j * NC + 1 - core, "chan": k}, device_id_type=MESH)
        return carry

    lax.fori_loop(0, NCH, greet_other, 0)

    lane = lax.broadcasted_iota(jnp.int32, (1, C), 1) // 64

    def mask_row(k):
        row = jnp.zeros((1, C), F32)
        for b in range(4):
            row = jnp.where(lane == b, pat_ref[k, c // 2, b].astype(F32), row)
        return row

    for k in range(4):
        row = mask_row(k)
        for p in range(2):
            wmask[k, p] = (w_ref[k, p].astype(F32) * row).astype(BF16)

    xf[0:1024, :] = x_ref[...].reshape(1024, 128).astype(F32)
    xf[1024:2048, :] = g_ref[...].reshape(1024, 128).astype(F32)
    for s in range(S):
        rows = [xf[pl.ds(q * 1024 + p * S + s, CH, stride=2 * S), :] for q in range(2) for p in range(2)]
        b32[pl.ds(s, 128, stride=S), :] = jnp.concatenate(rows, axis=0).T
    sbuf[...] = b32[...].reshape(128, S, 128).astype(BF16)

    pl.semaphore_wait(barrier, NCHIP - 1 + NCH)

    w_self = c // 4 == core
    for k in range(4):
        for other in range(NC):
            mine = (4 * core + k == c) & (core == other)

            @pl.when(mine)
            def _():
                pltpu.make_async_copy(wmask.at[k], wrecv.at[c], w_recv).start()

            @pl.when(jnp.logical_not(mine))
            def _():
                pltpu.make_async_remote_copy(
                    src_ref=wmask.at[k], dst_ref=wrecv.at[c], send_sem=w_send, recv_sem=w_recv,
                    device_id={"blk": j * NC + other, "chan": 4 * core + k}, device_id_type=MESH).start()

    def send_x(t, carry):
        tj, tc = at(t)
        pltpu.make_async_remote_copy(
            src_ref=sbuf.at[tj * NCH + tc], dst_ref=xm.at[c, pl.ds(pl.multiple_of(j * S, S), S)],
            send_sem=x_send, recv_sem=x_recv,
            device_id={"blk": tj * NC + core, "chan": tc}, device_id_type=MESH).start()
        return carry

    lax.fori_loop(1, NCHIP, send_x, 0)
    own_x = pltpu.make_async_copy(sbuf.at[j * NCH + c], xm.at[c, pl.ds(pl.multiple_of(j * S, S), S)], x_loc)
    own_x.start()

    for q in range(4):
        o = lax.broadcasted_iota(jnp.int32, (C, NCH * 128), 0)
        l = lax.broadcasted_iota(jnp.int32, (C, NCH * 128), 1)
        ebuf[q] = (l == (o // CH) * 128 + q * CH + o % CH).astype(F32).astype(BF16)

    pltpu.make_async_copy(wrecv, wrecv, w_recv).wait()
    wr = wrecv[:, 0].reshape(C, C)
    wi = wrecv[:, 1].reshape(C, C)
    wrt = wr.astype(F32).T.astype(BF16)
    wit = wi.astype(F32).T.astype(BF16)

    def spread(a, qa, b, qb):
        left = jnp.dot(a, ebuf[qa], preferred_element_type=F32)
        return (left + jnp.dot(b, ebuf[qb], preferred_element_type=F32)).astype(BF16)

    for part, rows in enumerate((spread(wr, 0, wi, 1), spread(-wi, 0, wr, 1),
                                 spread(wrt, 2, -wit, 3), spread(wit, 2, wrt, 3))):
        for k in range(NCH):
            wb[k * 128 + part * CH:k * 128 + part * CH + CH, :] = rows[k * CH:(k + 1) * CH, :]

    own_x.wait()
    pltpu.make_async_copy(sbuf.at[pl.ds(0, NCHIP - 1)], sbuf.at[pl.ds(0, NCHIP - 1)], x_recv).wait()
    full = jnp.concatenate([xm[k] for k in range(NCH)], axis=1)
    for n in range(4):
        part = jnp.dot(full, wb[:, n * 256:(n + 1) * 256], preferred_element_type=F32).astype(BF16)
        ybuf[2 * n] = part[:, :128]
        ybuf[2 * n + 1] = part[:, 128:]

    def send_y(t, carry):
        tj, tc = at(t)
        pltpu.make_async_remote_copy(
            src_ref=ybuf.at[tc, pl.ds(pl.multiple_of(tj * S, S), S)], dst_ref=rbuf.at[j * NCH + c],
            send_sem=y_send, recv_sem=y_recv,
            device_id={"blk": tj * NC + core, "chan": tc}, device_id_type=MESH).start()
        return carry

    lax.fori_loop(1, NCHIP, send_y, 0)
    own_y = pltpu.make_async_copy(ybuf.at[c, pl.ds(pl.multiple_of(j * S, S), S)], rbuf.at[j * NCH + c], y_loc)
    own_y.start()

    for h in range(2):
        gall[:, h * C:(h + 1) * C] = lax.dot_general(
            full, ebuf[2 + h], (((1,), (1,)), ((), ())), preferred_element_type=F32).astype(BF16)
    for k in range(NCH):
        both = lax.dot_general(xm[k], gall[...], (((0,), (0,)), ((), ())), preferred_element_type=F32)
        gwbuf[k, 0] = both[0:CH, :C] + both[CH:2 * CH, C:]
        gwbuf[k, 1] = both[0:CH, C:] - both[CH:2 * CH, :C]

    for k in range(NCH):
        mine = w_self & (c == k)

        @pl.when(mine)
        def _():
            pltpu.make_async_copy(gwbuf.at[k], gwr.at[core, c % 4], d_recv).start()

        @pl.when(jnp.logical_not(mine))
        def _():
            pltpu.make_async_remote_copy(
                src_ref=gwbuf.at[k], dst_ref=gwr.at[core, c % 4], send_sem=d_send, recv_sem=d_recv,
                device_id={"blk": j * NC + c // 4, "chan": k}, device_id_type=MESH).start()

    own_y.wait()
    pltpu.make_async_copy(rbuf.at[pl.ds(0, NCHIP - 1)], rbuf.at[pl.ds(0, NCHIP - 1)], y_recv).wait()
    b32[...] = rbuf[...].astype(F32).reshape(2048, 128)
    for s in range(S):
        tile = b32[pl.ds(s, 128, stride=S), :].T
        for q in range(2):
            for p in range(2):
                at_row = (2 * q + p) * CH
                xf[pl.ds(q * 1024 + p * S + s, CH, stride=2 * S), :] = tile[at_row:at_row + CH]
    out_ref[...] = xf[0:1024, :].astype(BF16).reshape(CH, 2, S, 128)
    gin_ref[...] = xf[1024:2048, :].astype(BF16).reshape(CH, 2, S, 128)

    pltpu.make_async_copy(gwr, gwr, d_recv).wait()
    for k in range(4):
        row = mask_row(k)
        for p in range(2):
            gw_ref[k, p] = (gwr[0, k, p] + gwr[1, k, p]) * row

    def sent(buf, sem):
        pltpu.make_async_copy(buf, buf, sem).wait()

    sent(sbuf.at[pl.ds(0, NCHIP - 1)], x_send)
    sent(rbuf.at[pl.ds(0, NCHIP - 1)], y_send)

    @pl.when(w_self)
    def _():
        sent(wrecv.at[pl.ds(0, NCH - 1)], w_send)
        sent(gwbuf.at[pl.ds(0, NCH - 1)], d_send)

    @pl.when(jnp.logical_not(w_self))
    def _():
        sent(wrecv, w_send)
        sent(gwbuf, d_send)


def local(spec_in, weight, pattern, cotangent):
    vmem = pl.BlockSpec(memory_space=pltpu.VMEM)
    dma = pltpu.SemaphoreType.DMA
    return pl.pallas_call(
        kernel,
        out_shape=(
            jax.ShapeDtypeStruct(spec_in.shape, BF16),
            jax.ShapeDtypeStruct(spec_in.shape, BF16),
            jax.ShapeDtypeStruct(weight.shape, F32),
        ),
        in_specs=[vmem, vmem, pl.BlockSpec(memory_space=pltpu.SMEM), vmem],
        out_specs=(vmem, vmem, vmem),
        scratch_shapes=[
            pltpu.VMEM((2048, 128), F32),
            pltpu.VMEM((2048, 128), F32),
            pltpu.VMEM((NCHIP, S, 128), BF16),
            pltpu.VMEM((NCH, NJ * S, 128), BF16),
            pltpu.VMEM((4, 2, CH, C), BF16),
            pltpu.VMEM((NCH, 2, CH, C), BF16),
            pltpu.VMEM((NCH * 128, NCH * 128), BF16),
            pltpu.VMEM((4, C, NCH * 128), BF16),
            pltpu.VMEM((NCH, NJ * S, 128), BF16),
            pltpu.VMEM((NCHIP, S, 128), BF16),
            pltpu.VMEM((NJ * S, 2 * C), BF16),
            pltpu.VMEM((NCH, 2, CH, C), F32),
            pltpu.VMEM((NC, 4, 2, CH, C), F32),
        ] + [dma] * 10,
        compiler_params=pltpu.CompilerParams(
            collective_id=0, has_side_effects=True, vmem_limit_bytes=48 << 20),
    )(spec_in, weight, pattern, cotangent)


def solution(mesh):
    in_specs = (
        P("chan", None, "blk", None),
        P("blk", None, "chan", None),
        P("blk", None, None),
        P("chan", None, "blk", None),
    )
    out_specs = (
        P("chan", None, "blk", None),
        P("chan", None, "blk", None),
        P("blk", None, "chan", None),
    )
    return jax.shard_map(local, mesh=mesh, in_specs=in_specs, out_specs=out_specs, check_vma=False)
```

```python
import jax
import jax.numpy as jnp
from jax import lax
from jax.experimental import pallas as pl
from jax.experimental.pallas import tpu as pltpu
from jax.sharding import PartitionSpec as P

F32 = jnp.float32
BF16 = jnp.bfloat16
MESH = pl.DeviceIdType.MESH

NZ, NYL, NC, NYH, NX = 8, 2, 2, 2, 4
NJ = NZ * NYL
NCH = NYH * NX
NCHIP = NJ * NCH
NXY = NCHIP // NZ
CH = 32
S = 16
C = 256
SLOT = NYL * S

OFFSETS = (4, 3, 5, 2, 6, 1, 7, 0)
GROUPS = ((0, 3), (3, 8))


def kernel(x_hbm, w_hbm, pat_hbm, g_hbm, rbuf, gwr, mask_ref,
           xv, gv, wv, pat_ref, xf, b32, sbuf, xm, wmask, wrecv, wb, ebuf, ybuf, gall, gwbuf,
           known, in_x, in_g, in_w, in_p, x_send, x_recv0, x_recv1, x_loc,
           w_send, w_recv, y_send, y_recv, y_loc, d_send, d_recv):
    blk = lax.axis_index("blk")
    c = lax.axis_index("chan")
    core = blk & 1
    j = blk >> 1
    z = j >> 1
    y = (c >> 2) * NYL + (j & 1)
    x = c & 3
    x_recv = (x_recv0, x_recv1)

    fetch_x = pltpu.make_async_copy(x_hbm, xv, in_x)
    fetch_g = pltpu.make_async_copy(g_hbm, gv, in_g)
    fetch_w = pltpu.make_async_copy(w_hbm, wv, in_w)
    fetch_p = pltpu.make_async_copy(pat_hbm, pat_ref, in_p)
    fetch_p.start()
    fetch_w.start()
    fetch_x.start()
    fetch_g.start()

    barrier = pltpu.get_barrier_semaphore()

    def signal(sem, b, k):
        pl.semaphore_signal(sem, inc=1, device_id={"blk": b, "chan": k}, device_id_type=MESH)

    def greet_j(t, carry):
        signal(barrier, ((j ^ t) << 1) + core, c)
        return carry

    def greet_c(t, carry):
        signal(barrier, blk, c ^ t)
        return carry

    def greet_core(t, carry):
        signal(barrier, blk ^ 1, c ^ t)
        return carry

    lax.fori_loop(1, NJ, greet_j, 0)
    lax.fori_loop(1, NCH, greet_c, 0)
    lax.fori_loop(0, NCH, greet_core, 0)

    lane = lax.broadcasted_iota(jnp.int32, (1, C), 1) // 64
    fetch_p.wait()
    fetch_w.wait()
    for k in range(4):
        row = jnp.zeros((1, C), F32)
        for b in range(4):
            row = jnp.where(lane == b, pat_ref[k, c >> 1, b].astype(F32), row)
        mask_ref[k:k + 1, :] = row
        for p in range(2):
            wmask[k, p] = (wv[k, p].astype(F32) * row).astype(BF16)

    fetch_x.wait()
    fetch_g.wait()
    xf[0:1024, :] = xv[...].reshape(1024, 128).astype(F32)
    xf[1024:2048, :] = gv[...].reshape(1024, 128).astype(F32)
    for s in range(S):
        rows = [xf[pl.ds(q * 1024 + p * S + s, CH, stride=2 * S), :] for q in range(2) for p in range(2)]
        b32[pl.ds(s, 128, stride=S), :] = jnp.concatenate(rows, axis=0).T
    sbuf[...] = b32[...].reshape(128, S, 128).astype(BF16)

    pl.semaphore_wait(barrier, NJ - 1 + NCH - 1 + NCH)

    def tell(t, carry):
        signal(known, blk, c ^ t)
        return carry

    lax.fori_loop(1, NCH, tell, 0)
    pl.semaphore_wait(known, NCH - 1)

    def xy(u):
        ty = (y + (u & 3)) & 3
        tx = (x + (u >> 2)) & 3
        return ty & 1, (ty >> 1) * NX + tx

    def rows_of(slot, yl):
        return pl.ds(pl.multiple_of(slot * SLOT + yl * S, S), S)

    own_rows = rows_of(NZ - 1, j & 1)

    def send_x(g, slot, u):
        yl, tc = xy(u)
        tj = ((z + OFFSETS[slot]) & 7) * NYL + yl
        pltpu.make_async_remote_copy(
            src_ref=sbuf.at[tj * NCH + tc], dst_ref=xm.at[c, rows_of(slot, j & 1)],
            send_sem=x_send, recv_sem=x_recv[g],
            device_id={"blk": tj * NC + core, "chan": tc}, device_id_type=MESH).start()

    def send_y(slot, u):
        yl, tc = xy(u)
        tj = ((z - OFFSETS[slot]) & 7) * NYL + yl
        pltpu.make_async_remote_copy(
            src_ref=ybuf.at[tc, rows_of(slot, yl)], dst_ref=rbuf.at[j * NCH + c],
            send_sem=y_send, recv_sem=y_recv,
            device_id={"blk": tj * NC + core, "chan": tc}, device_id_type=MESH).start()

    def send_group(g, send):
        first, last = GROUPS[g]

        def step(u, carry):
            for slot in range(first, min(last, NZ - 1)):
                send(slot, u)
            return carry

        lax.fori_loop(0, NXY, step, 0)
        if last == NZ:
            def plane(u, carry):
                send(NZ - 1, u)
                return carry

            lax.fori_loop(1, NXY, plane, 0)

    send_group(0, lambda slot, u: send_x(0, slot, u))

    w_self = (c >> 2) == core
    for k in range(4):
        for other in range(NC):
            mine = (4 * core + k == c) & (core == other)

            @pl.when(mine)
            def _():
                pltpu.make_async_copy(wmask.at[k], wrecv.at[c], w_recv).start()

            @pl.when(jnp.logical_not(mine))
            def _():
                pltpu.make_async_remote_copy(
                    src_ref=wmask.at[k], dst_ref=wrecv.at[c], send_sem=w_send, recv_sem=w_recv,
                    device_id={"blk": j * NC + other, "chan": 4 * core + k}, device_id_type=MESH).start()

    send_group(1, lambda slot, u: send_x(1, slot, u))
    own_x = pltpu.make_async_copy(sbuf.at[j * NCH + c], xm.at[c, own_rows], x_loc)
    own_x.start()

    for q in range(4):
        o = lax.broadcasted_iota(jnp.int32, (C, NCH * 128), 0)
        l = lax.broadcasted_iota(jnp.int32, (C, NCH * 128), 1)
        ebuf[q] = (l == (o // CH) * 128 + q * CH + o % CH).astype(F32).astype(BF16)

    pltpu.make_async_copy(wrecv, wrecv, w_recv).wait()
    wr = wrecv[:, 0].reshape(C, C)
    wi = wrecv[:, 1].reshape(C, C)
    wrt = wr.astype(F32).T.astype(BF16)
    wit = wi.astype(F32).T.astype(BF16)

    def spread(a, qa, b, qb):
        left = jnp.dot(a, ebuf[qa], preferred_element_type=F32)
        return (left + jnp.dot(b, ebuf[qb], preferred_element_type=F32)).astype(BF16)

    for part, rows in enumerate((spread(wr, 0, wi, 1), spread(-wi, 0, wr, 1),
                                 spread(wrt, 2, -wit, 3), spread(wit, 2, wrt, 3))):
        for k in range(NCH):
            wb[k * 128 + part * CH:k * 128 + part * CH + CH, :] = rows[k * CH:(k + 1) * CH, :]

    def load(lo, hi):
        return jnp.concatenate([xm[k, lo:hi] for k in range(NCH)], axis=1)

    def spread_grads(lo, hi):
        for h in range(2):
            gall[lo:hi, h * C:(h + 1) * C] = lax.dot_general(
                load(lo, hi), ebuf[2 + h], (((1,), (1,)), ((), ())), preferred_element_type=F32).astype(BF16)

    def products(lo, hi):
        rows = load(lo, hi)
        for n in range(4):
            part = jnp.dot(rows, wb[:, n * 256:(n + 1) * 256], preferred_element_type=F32).astype(BF16)
            ybuf[2 * n, lo:hi] = part[:, :128]
            ybuf[2 * n + 1, lo:hi] = part[:, 128:]

    cut = GROUPS[0][1] * SLOT

    def arrived(n, sem):
        pltpu.make_async_copy(sbuf.at[pl.ds(0, n)], sbuf.at[pl.ds(0, n)], sem).wait()

    arrived(GROUPS[0][1] * NXY, x_recv0)
    products(0, cut)
    send_group(0, send_y)
    spread_grads(0, cut)

    own_x.wait()
    arrived(NCHIP - 1 - GROUPS[0][1] * NXY, x_recv1)

    spread_grads(cut, NZ * SLOT)
    for k in range(NCH):
        both = lax.dot_general(xm[k], gall[...], (((0,), (0,)), ((), ())), preferred_element_type=F32)
        gwbuf[k, 0] = both[0:CH, :C] + both[CH:2 * CH, C:]
        gwbuf[k, 1] = both[0:CH, C:] - both[CH:2 * CH, :C]

    for k in range(NCH):
        mine = w_self & (c == k)

        @pl.when(mine)
        def _():
            pltpu.make_async_copy(gwbuf.at[k], gwr.at[core, c & 3], d_recv).start()

        @pl.when(jnp.logical_not(mine))
        def _():
            pltpu.make_async_remote_copy(
                src_ref=gwbuf.at[k], dst_ref=gwr.at[core, c & 3], send_sem=d_send, recv_sem=d_recv,
                device_id={"blk": j * NC + (c >> 2), "chan": k}, device_id_type=MESH).start()

    products(cut, NZ * SLOT)
    send_group(1, send_y)
    own_y = pltpu.make_async_copy(ybuf.at[c, own_rows], rbuf.at[j * NCH + c], y_loc)
    own_y.start()

    def done(buf, sem):
        pltpu.make_async_copy(buf, buf, sem).wait()

    @pl.when(w_self)
    def _():
        done(wrecv.at[pl.ds(0, NCH - 1)], w_send)
        done(gwbuf.at[pl.ds(0, NCH - 1)], d_send)

    @pl.when(jnp.logical_not(w_self))
    def _():
        done(wrecv, w_send)
        done(gwbuf, d_send)

    arrived(NCHIP - 1, x_send)
    arrived(NCHIP - 1, y_send)
    own_y.wait()
    done(gwbuf, d_recv)
    arrived(NCHIP - 1, y_recv)


def finish(rbuf, gwr, mask_ref, out_hbm, gin_hbm, gw_hbm, b32, xf, outv, ginv, gwv, s_out, s_gin, s_gw):
    for k in range(4):
        for p in range(2):
            gwv[k, p] = (gwr[0, k, p] + gwr[1, k, p]) * mask_ref[k:k + 1, :]
    put_gw = pltpu.make_async_copy(gwv, gw_hbm, s_gw)
    put_gw.start()

    b32[...] = rbuf[...].astype(F32).reshape(2048, 128)
    for s in range(S):
        tile = b32[pl.ds(s, 128, stride=S), :].T
        for q in range(2):
            for p in range(2):
                row = (2 * q + p) * CH
                xf[pl.ds(q * 1024 + p * S + s, CH, stride=2 * S), :] = tile[row:row + CH]
    outv[...] = xf[0:1024, :].astype(BF16).reshape(CH, 2, S, 128)
    put_out = pltpu.make_async_copy(outv, out_hbm, s_out)
    put_out.start()
    ginv[...] = xf[1024:2048, :].astype(BF16).reshape(CH, 2, S, 128)
    put_gin = pltpu.make_async_copy(ginv, gin_hbm, s_gin)
    put_gin.start()
    put_gw.wait()
    put_out.wait()
    put_gin.wait()


def local(spec_in, weight, pattern, cotangent):
    vmem = pl.BlockSpec(memory_space=pltpu.VMEM)
    hbm = pl.BlockSpec(memory_space=pltpu.HBM)
    dma = pltpu.SemaphoreType.DMA
    tiles, sums, mask = pl.pallas_call(
        kernel,
        out_shape=(
            jax.ShapeDtypeStruct((NCHIP, S, 128), BF16),
            jax.ShapeDtypeStruct((NC, 4, 2, CH, C), F32),
            jax.ShapeDtypeStruct((4, C), F32),
        ),
        in_specs=[hbm, hbm, hbm, hbm],
        out_specs=(vmem, vmem, vmem),
        scratch_shapes=[
            pltpu.VMEM(spec_in.shape, BF16),
            pltpu.VMEM(spec_in.shape, BF16),
            pltpu.VMEM(weight.shape, BF16),
            pltpu.SMEM(pattern.shape, jnp.int32),
            pltpu.VMEM((2048, 128), F32),
            pltpu.VMEM((2048, 128), F32),
            pltpu.VMEM((NCHIP, S, 128), BF16),
            pltpu.VMEM((NCH, NZ * SLOT, 128), BF16),
            pltpu.VMEM((4, 2, CH, C), BF16),
            pltpu.VMEM((NCH, 2, CH, C), BF16),
            pltpu.VMEM((NCH * 128, NCH * 128), BF16),
            pltpu.VMEM((4, C, NCH * 128), BF16),
            pltpu.VMEM((NCH, NZ * SLOT, 128), BF16),
            pltpu.VMEM((NZ * SLOT, 2 * C), BF16),
            pltpu.VMEM((NCH, 2, CH, C), F32),
            pltpu.SemaphoreType.REGULAR,
        ] + [dma] * 15,
        compiler_params=pltpu.CompilerParams(
            collective_id=0, has_side_effects=True, vmem_limit_bytes=40 << 20),
    )(*(pltpu.with_memory_space_constraint(a, pltpu.HBM) for a in (spec_in, weight, pattern, cotangent)))
    return pl.pallas_call(
        finish,
        out_shape=(
            jax.ShapeDtypeStruct(spec_in.shape, BF16),
            jax.ShapeDtypeStruct(spec_in.shape, BF16),
            jax.ShapeDtypeStruct(weight.shape, F32),
        ),
        in_specs=[vmem, vmem, vmem],
        out_specs=(hbm, hbm, hbm),
        scratch_shapes=[
            pltpu.VMEM((2048, 128), F32),
            pltpu.VMEM((2048, 128), F32),
            pltpu.VMEM(spec_in.shape, BF16),
            pltpu.VMEM(spec_in.shape, BF16),
            pltpu.VMEM(weight.shape, F32),
        ] + [dma] * 3,
        compiler_params=pltpu.CompilerParams(vmem_limit_bytes=16 << 20),
    )(tiles, sums, mask)


def solution(mesh):
    in_specs = (
        P("chan", None, "blk", None),
        P("blk", None, "chan", None),
        P("blk", None, None),
        P("chan", None, "blk", None),
    )
    out_specs = (
        P("chan", None, "blk", None),
        P("chan", None, "blk", None),
        P("blk", None, "chan", None),
    )
    return jax.shard_map(local, mesh=mesh, in_specs=in_specs, out_specs=out_specs, check_vma=False)
```

```python
import jax
import jax.numpy as jnp
from jax import lax
from jax.experimental import pallas as pl
from jax.experimental.pallas import tpu as pltpu
from jax.sharding import PartitionSpec as P

F32 = jnp.float32
BF16 = jnp.bfloat16
MESH = pl.DeviceIdType.MESH

NZ, NYL, NC, NYH, NX = 8, 2, 2, 2, 4
NJ = NZ * NYL
NCH = NYH * NX
NCHIP = NJ * NCH
NXY = NCHIP // NZ
CH = 32
S = 16
C = 256
SLOT = NYL * S

OFFSETS = (4, 3, 5, 2, 6, 1, 7, 0)
GROUPS = ((0, 3), (3, 8))


def kernel(x_hbm, w_hbm, pat_hbm, g_hbm, rbuf, gwr, mask_ref,
           xv, gv, wv, pat_ref, xf, b32, sbuf, xm, wmask, wrecv, wb, ebuf, ybuf, gall, gwbuf, gwx,
           known, in_x, in_g, in_w, in_p, x_send, x_recv0, x_recv1, x_loc,
           w_send, w_recv, h_send, h_recv, y_send, y_recv, y_loc, e_send, e_recv, d_send, d_recv):
    blk = lax.axis_index("blk")
    c = lax.axis_index("chan")
    core = blk & 1
    j = blk >> 1
    z = j >> 1
    y = (c >> 2) * NYL + (j & 1)
    x = c & 3
    x_recv = (x_recv0, x_recv1)

    fetch_x = pltpu.make_async_copy(x_hbm, xv, in_x)
    fetch_g = pltpu.make_async_copy(g_hbm, gv, in_g)
    fetch_w = pltpu.make_async_copy(w_hbm, wv, in_w)
    fetch_p = pltpu.make_async_copy(pat_hbm, pat_ref, in_p)
    fetch_p.start()
    fetch_w.start()
    fetch_x.start()
    fetch_g.start()

    barrier = pltpu.get_barrier_semaphore()

    def signal(sem, b, k):
        pl.semaphore_signal(sem, inc=1, device_id={"blk": b, "chan": k}, device_id_type=MESH)

    for t in range(1, NJ):
        signal(barrier, ((j ^ t) << 1) + core, c)
    for t in range(1, NCH):
        signal(barrier, blk, c ^ t)
    signal(barrier, blk ^ 1, c)

    lane = lax.broadcasted_iota(jnp.int32, (1, C), 1) // 64
    fetch_p.wait()
    fetch_w.wait()
    for k in range(4):
        row = jnp.zeros((1, C), F32)
        for b in range(4):
            row = jnp.where(lane == b, pat_ref[k, c >> 1, b].astype(F32), row)
        mask_ref[k:k + 1, :] = row
        for p in range(2):
            wmask[k, p] = (wv[k, p].astype(F32) * row).astype(BF16)

    pl.semaphore_wait(barrier, NJ - 1 + NCH - 1 + 1)
    for t in range(1, NCH):
        signal(known, blk, c ^ t)

    w_self = (c >> 2) == core
    for k in range(4):
        mine = 4 * core + k == c

        @pl.when(mine)
        def _():
            pltpu.make_async_copy(wmask.at[k], wrecv.at[c], w_recv).start()

        @pl.when(jnp.logical_not(mine))
        def _():
            pltpu.make_async_remote_copy(
                src_ref=wmask.at[k], dst_ref=wrecv.at[c], send_sem=w_send, recv_sem=w_recv,
                device_id={"blk": blk, "chan": 4 * core + k}, device_id_type=MESH).start()

    fetch_x.wait()
    fetch_g.wait()
    xf[0:1024, :] = xv[...].reshape(1024, 128).astype(F32)
    xf[1024:2048, :] = gv[...].reshape(1024, 128).astype(F32)
    for s in range(S):
        rows = [xf[pl.ds(q * 1024 + p * S + s, CH, stride=2 * S), :] for q in range(2) for p in range(2)]
        b32[pl.ds(s, 128, stride=S), :] = jnp.concatenate(rows, axis=0).T
    sbuf[...] = b32[...].reshape(128, S, 128).astype(BF16)

    def xy(u):
        ty = y ^ (u & 3)
        tx = (x + (u >> 2)) & 3
        return ty & 1, (ty >> 1) * NX + tx

    def rows_of(slot, yl):
        return pl.ds(pl.multiple_of(slot * SLOT + yl * S, S), S)

    own_rows = rows_of(NZ - 1, j & 1)

    def send_x(g, slot, u):
        yl, tc = xy(u)
        tj = ((z + OFFSETS[slot]) & 7) * NYL + yl
        pltpu.make_async_remote_copy(
            src_ref=sbuf.at[tj * NCH + tc], dst_ref=xm.at[c, rows_of(slot, j & 1)],
            send_sem=x_send, recv_sem=x_recv[g],
            device_id={"blk": tj * NC + core, "chan": tc}, device_id_type=MESH).start()

    def send_y(slot, u):
        yl, tc = xy(u)
        tj = ((z - OFFSETS[slot]) & 7) * NYL + yl
        pltpu.make_async_remote_copy(
            src_ref=ybuf.at[tc, rows_of(slot, yl)], dst_ref=rbuf.at[j * NCH + c],
            send_sem=y_send, recv_sem=y_recv,
            device_id={"blk": tj * NC + core, "chan": tc}, device_id_type=MESH).start()

    def send_slots(send, first, last, start, also=None):
        def step(u, carry):
            for slot in range(first, min(last, NZ - 1)):
                send(slot, u)
            if also is not None:
                also(u)
            return carry

        lax.fori_loop(start, NXY, step, 0)
        if last == NZ:
            def plane(u, carry):
                send(NZ - 1, u)
                return carry

            lax.fori_loop(max(start, 1), NXY, plane, 0)

    def send_group(g, send, start=0):
        send_slots(send, *GROUPS[g], start)

    for u in range(2):
        for g, (first, last) in enumerate(GROUPS):
            for slot in range(first, last - 1 if last == NZ and u == 0 else last):
                send_x(g, slot, u)
    pl.semaphore_wait(known, NCH - 1)
    send_group(0, lambda slot, u: send_x(0, slot, u), 2)
    send_group(1, lambda slot, u: send_x(1, slot, u), 2)
    own_x = pltpu.make_async_copy(sbuf.at[j * NCH + c], xm.at[c, own_rows], x_loc)
    own_x.start()

    for q in range(4):
        o = lax.broadcasted_iota(jnp.int32, (C, NCH * 128), 0)
        l = lax.broadcasted_iota(jnp.int32, (C, NCH * 128), 1)
        ebuf[q] = (l == (o // CH) * 128 + q * CH + o % CH).astype(F32).astype(BF16)

    hand_over = pltpu.make_async_remote_copy(
        src_ref=wrecv, dst_ref=wrecv, send_sem=h_send, recv_sem=h_recv,
        device_id={"blk": blk ^ 1, "chan": c}, device_id_type=MESH)

    @pl.when(w_self)
    def _():
        pltpu.make_async_copy(wrecv, wrecv, w_recv).wait()
        hand_over.start()

    @pl.when(jnp.logical_not(w_self))
    def _():
        hand_over.wait_recv()

    wr = wrecv[:, 0].reshape(C, C)
    wi = wrecv[:, 1].reshape(C, C)
    wrt = wr.astype(F32).T.astype(BF16)
    wit = wi.astype(F32).T.astype(BF16)

    def spread(a, qa, b, qb):
        left = jnp.dot(a, ebuf[qa], preferred_element_type=F32)
        return (left + jnp.dot(b, ebuf[qb], preferred_element_type=F32)).astype(BF16)

    for part, rows in enumerate((spread(wr, 0, wi, 1), spread(-wi, 0, wr, 1),
                                 spread(wrt, 2, -wit, 3), spread(wit, 2, wrt, 3))):
        for k in range(NCH):
            wb[k * 128 + part * CH:k * 128 + part * CH + CH, :] = rows[k * CH:(k + 1) * CH, :]

    def load(lo, hi):
        return jnp.concatenate([xm[k, lo:hi] for k in range(NCH)], axis=1)

    def spread_grads(lo, hi):
        for h in range(2):
            gall[lo:hi, h * C:(h + 1) * C] = lax.dot_general(
                load(lo, hi), ebuf[2 + h], (((1,), (1,)), ((), ())), preferred_element_type=F32).astype(BF16)

    def products(lo, hi):
        rows = load(lo, hi)
        for n in range(4):
            part = jnp.dot(rows, wb[:, n * 256:(n + 1) * 256], preferred_element_type=F32).astype(BF16)
            ybuf[2 * n, lo:hi] = part[:, :128]
            ybuf[2 * n + 1, lo:hi] = part[:, 128:]

    cut = GROUPS[0][1] * SLOT

    def arrived(n, sem):
        pltpu.make_async_copy(sbuf.at[pl.ds(0, n)], sbuf.at[pl.ds(0, n)], sem).wait()

    arrived(GROUPS[0][1] * NXY, x_recv0)
    products(0, cut)
    send_group(0, send_y)
    spread_grads(0, cut)

    own_x.wait()
    arrived(NCHIP - 1 - GROUPS[0][1] * NXY, x_recv1)

    products(cut, NZ * SLOT)
    send_slots(send_y, 3, 8, 0)
    spread_grads(cut, NZ * SLOT)
    theirs, ours = 4 * (1 - core), 4 * core

    def weight_grads(k):
        both = lax.dot_general(xm[k], gall[...], (((0,), (0,)), ((), ())), preferred_element_type=F32)
        gwbuf[k, 0] = both[0:CH, :C] + both[CH:2 * CH, C:]
        gwbuf[k, 1] = both[0:CH, C:] - both[CH:2 * CH, :C]

    for k in range(4):
        weight_grads(theirs + k)
    exchange = pltpu.make_async_remote_copy(
        src_ref=gwbuf.at[pl.ds(theirs, 4)], dst_ref=gwx, send_sem=e_send, recv_sem=e_recv,
        device_id={"blk": blk ^ 1, "chan": c}, device_id_type=MESH)
    exchange.start()
    for k in range(4):
        weight_grads(ours + k)
    exchange.wait_recv()
    for k in range(4):
        gwbuf[ours + k] += gwx[k]

    for k in range(4):
        mine = ours + k == c

        @pl.when(mine)
        def _():
            pltpu.make_async_copy(gwbuf.at[ours + k], gwr.at[c & 3], d_recv).start()

        @pl.when(jnp.logical_not(mine))
        def _():
            pltpu.make_async_remote_copy(
                src_ref=gwbuf.at[ours + k], dst_ref=gwr.at[c & 3], send_sem=d_send, recv_sem=d_recv,
                device_id={"blk": j * NC + (c >> 2), "chan": ours + k}, device_id_type=MESH).start()

    own_y = pltpu.make_async_copy(ybuf.at[c, own_rows], rbuf.at[j * NCH + c], y_loc)
    own_y.start()

    def done(buf, sem):
        pltpu.make_async_copy(buf, buf, sem).wait()

    @pl.when(w_self)
    def _():
        done(wrecv.at[pl.ds(0, 3)], w_send)
        hand_over.wait_send()
        done(gwr.at[pl.ds(0, 3)], d_send)

    @pl.when(jnp.logical_not(w_self))
    def _():
        done(wrecv.at[pl.ds(0, 4)], w_send)
        done(gwr, d_send)

    arrived(NCHIP - 1, x_send)
    arrived(NCHIP - 1, y_send)
    own_y.wait()
    exchange.wait_send()
    done(gwr, d_recv)
    arrived(NCHIP - 1, y_recv)


def finish(rbuf, gwr, mask_ref, out_hbm, gin_hbm, gw_hbm, b32, xf, outv, ginv, gwv, s_out, s_gin, s_gw):
    for k in range(4):
        for p in range(2):
            gwv[k, p] = gwr[k, p] * mask_ref[k:k + 1, :]
    put_gw = pltpu.make_async_copy(gwv, gw_hbm, s_gw)
    put_gw.start()

    b32[...] = rbuf[...].astype(F32).reshape(2048, 128)
    for s in range(S):
        tile = b32[pl.ds(s, 128, stride=S), :].T
        for q in range(2):
            for p in range(2):
                row = (2 * q + p) * CH
                xf[pl.ds(q * 1024 + p * S + s, CH, stride=2 * S), :] = tile[row:row + CH]
    outv[...] = xf[0:1024, :].astype(BF16).reshape(CH, 2, S, 128)
    put_out = pltpu.make_async_copy(outv, out_hbm, s_out)
    put_out.start()
    ginv[...] = xf[1024:2048, :].astype(BF16).reshape(CH, 2, S, 128)
    put_gin = pltpu.make_async_copy(ginv, gin_hbm, s_gin)
    put_gin.start()
    put_gw.wait()
    put_out.wait()
    put_gin.wait()


def local(spec_in, weight, pattern, cotangent):
    vmem = pl.BlockSpec(memory_space=pltpu.VMEM)
    hbm = pl.BlockSpec(memory_space=pltpu.HBM)
    dma = pltpu.SemaphoreType.DMA
    tiles, sums, mask = pl.pallas_call(
        kernel,
        out_shape=(
            jax.ShapeDtypeStruct((NCHIP, S, 128), BF16),
            jax.ShapeDtypeStruct(weight.shape, F32),
            jax.ShapeDtypeStruct((4, C), F32),
        ),
        in_specs=[hbm, hbm, hbm, hbm],
        out_specs=(vmem, vmem, vmem),
        scratch_shapes=[
            pltpu.VMEM(spec_in.shape, BF16),
            pltpu.VMEM(spec_in.shape, BF16),
            pltpu.VMEM(weight.shape, BF16),
            pltpu.SMEM(pattern.shape, jnp.int32),
            pltpu.VMEM((2048, 128), F32),
            pltpu.VMEM((2048, 128), F32),
            pltpu.VMEM((NCHIP, S, 128), BF16),
            pltpu.VMEM((NCH, NZ * SLOT, 128), BF16),
            pltpu.VMEM((4, 2, CH, C), BF16),
            pltpu.VMEM((NCH, 2, CH, C), BF16),
            pltpu.VMEM((NCH * 128, NCH * 128), BF16),
            pltpu.VMEM((4, C, NCH * 128), BF16),
            pltpu.VMEM((NCH, NZ * SLOT, 128), BF16),
            pltpu.VMEM((NZ * SLOT, 2 * C), BF16),
            pltpu.VMEM((NCH, 2, CH, C), F32),
            pltpu.VMEM(weight.shape, F32),
            pltpu.SemaphoreType.REGULAR,
        ] + [dma] * 19,
        compiler_params=pltpu.CompilerParams(
            collective_id=0, has_side_effects=True, vmem_limit_bytes=40 << 20),
    )(*(pltpu.with_memory_space_constraint(a, pltpu.HBM) for a in (spec_in, weight, pattern, cotangent)))
    return pl.pallas_call(
        finish,
        out_shape=(
            jax.ShapeDtypeStruct(spec_in.shape, BF16),
            jax.ShapeDtypeStruct(spec_in.shape, BF16),
            jax.ShapeDtypeStruct(weight.shape, F32),
        ),
        in_specs=[vmem, vmem, vmem],
        out_specs=(hbm, hbm, hbm),
        scratch_shapes=[
            pltpu.VMEM((2048, 128), F32),
            pltpu.VMEM((2048, 128), F32),
            pltpu.VMEM(spec_in.shape, BF16),
            pltpu.VMEM(spec_in.shape, BF16),
            pltpu.VMEM(weight.shape, F32),
        ] + [dma] * 3,
        compiler_params=pltpu.CompilerParams(vmem_limit_bytes=16 << 20),
    )(tiles, sums, mask)


def solution(mesh):
    in_specs = (
        P("chan", None, "blk", None),
        P("blk", None, "chan", None),
        P("blk", None, None),
        P("chan", None, "blk", None),
    )
    out_specs = (
        P("chan", None, "blk", None),
        P("chan", None, "blk", None),
        P("blk", None, "chan", None),
    )
    return jax.shard_map(local, mesh=mesh, in_specs=in_specs, out_specs=out_specs, check_vma=False)
```

```python
import jax
import jax.numpy as jnp
from jax import lax
from jax.experimental import pallas as pl
from jax.experimental.pallas import tpu as pltpu
from jax.sharding import PartitionSpec as P

F32 = jnp.float32
BF16 = jnp.bfloat16
MESH = pl.DeviceIdType.MESH

NZ, NYL, NC, NYH, NX = 8, 2, 2, 2, 4
NJ = NZ * NYL
NCH = NYH * NX
NCHIP = NJ * NCH
NXY = NCHIP // NZ
CH = 32
S = 16
C = 256
SLOT = NYL * S

OFFSETS = (4, 3, 5, 2, 6, 1, 7, 0)
GROUPS = ((0, 3), (3, 8))


def kernel(x_hbm, w_hbm, pat_hbm, g_hbm, rbuf, gwr, mask_ref,
           xv, gv, wv, pat_ref, xf, b32, sbuf, xm, wmask, wrecv, wb, ebuf, ybuf, gall, gwbuf, gwx,
           known, in_x, in_g, in_w, in_p, x_send, x_recv0, x_recv1, x_loc,
           w_send, w_recv, h_send, h_recv, y_send, y_recv, y_loc, e_send, e_recv, d_send, d_recv):
    blk = lax.axis_index("blk")
    c = lax.axis_index("chan")
    core = blk & 1
    j = blk >> 1
    z = j >> 1
    y = (c >> 2) * NYL + (j & 1)
    x = c & 3
    x_recv = (x_recv0, x_recv1)

    fetch_x = pltpu.make_async_copy(x_hbm, xv, in_x)
    fetch_g = pltpu.make_async_copy(g_hbm, gv, in_g)
    fetch_w = pltpu.make_async_copy(w_hbm, wv, in_w)
    fetch_p = pltpu.make_async_copy(pat_hbm, pat_ref, in_p)
    fetch_p.start()
    fetch_w.start()
    fetch_x.start()
    fetch_g.start()

    barrier = pltpu.get_barrier_semaphore()

    def signal(sem, b, k):
        pl.semaphore_signal(sem, inc=1, device_id={"blk": b, "chan": k}, device_id_type=MESH)

    for t in range(1, NJ):
        signal(barrier, ((j ^ t) << 1) + core, c)
    for t in range(1, NCH):
        signal(barrier, blk, c ^ t)
    signal(barrier, blk ^ 1, c)

    lane = lax.broadcasted_iota(jnp.int32, (1, C), 1) // 64
    fetch_p.wait()
    fetch_w.wait()
    for k in range(4):
        row = jnp.zeros((1, C), F32)
        for b in range(4):
            row = jnp.where(lane == b, pat_ref[k, c >> 1, b].astype(F32), row)
        mask_ref[k:k + 1, :] = row
        for p in range(2):
            wmask[k, p] = (wv[k, p].astype(F32) * row).astype(BF16)

    pl.semaphore_wait(barrier, NJ - 1 + NCH - 1 + 1)
    for t in range(1, NCH):
        signal(known, blk, c ^ t)

    w_self = (c >> 2) == core
    for k in range(4):
        mine = 4 * core + k == c

        @pl.when(mine)
        def _():
            pltpu.make_async_copy(wmask.at[k], wrecv.at[c], w_recv).start()

        @pl.when(jnp.logical_not(mine))
        def _():
            pltpu.make_async_remote_copy(
                src_ref=wmask.at[k], dst_ref=wrecv.at[c], send_sem=w_send, recv_sem=w_recv,
                device_id={"blk": blk, "chan": 4 * core + k}, device_id_type=MESH).start()

    fetch_x.wait()
    fetch_g.wait()
    xf[0:1024, :] = xv[...].reshape(1024, 128).astype(F32)
    xf[1024:2048, :] = gv[...].reshape(1024, 128).astype(F32)
    for s in range(S):
        rows = [xf[pl.ds(q * 1024 + p * S + s, CH, stride=2 * S), :] for q in range(2) for p in range(2)]
        b32[pl.ds(s, 128, stride=S), :] = jnp.concatenate(rows, axis=0).T
    sbuf[...] = b32[...].reshape(128, S, 128).astype(BF16)

    def xy(u):
        ty = y ^ (u & 3)
        tx = (x + (u >> 2)) & 3
        return ty & 1, (ty >> 1) * NX + tx

    def rows_of(slot, yl):
        return pl.ds(pl.multiple_of(slot * SLOT + yl * S, S), S)

    own_rows = rows_of(NZ - 1, j & 1)

    def send_x(g, slot, u):
        yl, tc = xy(u)
        tj = ((z + OFFSETS[slot]) & 7) * NYL + yl
        pltpu.make_async_remote_copy(
            src_ref=sbuf.at[tj * NCH + tc], dst_ref=xm.at[c, rows_of(slot, j & 1)],
            send_sem=x_send, recv_sem=x_recv[g],
            device_id={"blk": tj * NC + core, "chan": tc}, device_id_type=MESH).start()

    def send_y(slot, u):
        yl, tc = xy(u)
        tj = ((z - OFFSETS[slot]) & 7) * NYL + yl
        pltpu.make_async_remote_copy(
            src_ref=ybuf.at[tc, rows_of(slot, yl)], dst_ref=rbuf.at[j * NCH + c],
            send_sem=y_send, recv_sem=y_recv,
            device_id={"blk": tj * NC + core, "chan": tc}, device_id_type=MESH).start()

    def send_slots(send, first, last, start, also=None):
        def step(u, carry):
            for slot in range(first, min(last, NZ - 1)):
                send(slot, u)
            if also is not None:
                also(u)
            return carry

        lax.fori_loop(start, NXY, step, 0)
        if last == NZ:
            def plane(u, carry):
                send(NZ - 1, u)
                return carry

            lax.fori_loop(max(start, 1), NXY, plane, 0)

    def send_group(g, send, start=0):
        send_slots(send, *GROUPS[g], start)

    for u in range(2):
        for g, (first, last) in enumerate(GROUPS):
            for slot in range(first, last - 1 if last == NZ and u == 0 else last):
                send_x(g, slot, u)
    pl.semaphore_wait(known, NCH - 1)
    send_group(0, lambda slot, u: send_x(0, slot, u), 2)
    send_group(1, lambda slot, u: send_x(1, slot, u), 2)
    own_x = pltpu.make_async_copy(sbuf.at[j * NCH + c], xm.at[c, own_rows], x_loc)
    own_x.start()

    for q in range(4):
        o = lax.broadcasted_iota(jnp.int32, (C, NCH * 128), 0)
        l = lax.broadcasted_iota(jnp.int32, (C, NCH * 128), 1)
        ebuf[q] = (l == (o // CH) * 128 + q * CH + o % CH).astype(F32).astype(BF16)

    hand_over = pltpu.make_async_remote_copy(
        src_ref=wrecv, dst_ref=wrecv, send_sem=h_send, recv_sem=h_recv,
        device_id={"blk": blk ^ 1, "chan": c}, device_id_type=MESH)

    @pl.when(w_self)
    def _():
        pltpu.make_async_copy(wrecv, wrecv, w_recv).wait()
        hand_over.start()

    @pl.when(jnp.logical_not(w_self))
    def _():
        hand_over.wait_recv()

    wr = wrecv[:, 0].reshape(C, C)
    wi = wrecv[:, 1].reshape(C, C)
    wrt = wr.astype(F32).T.astype(BF16)
    wit = wi.astype(F32).T.astype(BF16)

    def spread(a, qa, b, qb):
        left = jnp.dot(a, ebuf[qa], preferred_element_type=F32)
        return (left + jnp.dot(b, ebuf[qb], preferred_element_type=F32)).astype(BF16)

    for part, rows in enumerate((spread(wr, 0, wi, 1), spread(-wi, 0, wr, 1),
                                 spread(wrt, 2, -wit, 3), spread(wit, 2, wrt, 3))):
        for k in range(NCH):
            wb[k * 128 + part * CH:k * 128 + part * CH + CH, :] = rows[k * CH:(k + 1) * CH, :]

    def load(lo, hi):
        return jnp.concatenate([xm[k, lo:hi] for k in range(NCH)], axis=1)

    def spread_grads(lo, hi):
        for h in range(2):
            gall[lo:hi, h * C:(h + 1) * C] = lax.dot_general(
                load(lo, hi), ebuf[2 + h], (((1,), (1,)), ((), ())), preferred_element_type=F32).astype(BF16)

    def products(lo, hi):
        rows = load(lo, hi)
        for n in range(4):
            part = jnp.dot(rows, wb[:, n * 256:(n + 1) * 256], preferred_element_type=F32).astype(BF16)
            ybuf[2 * n, lo:hi] = part[:, :128]
            ybuf[2 * n + 1, lo:hi] = part[:, 128:]

    cut = GROUPS[0][1] * SLOT

    def arrived(n, sem):
        pltpu.make_async_copy(sbuf.at[pl.ds(0, n)], sbuf.at[pl.ds(0, n)], sem).wait()

    arrived(GROUPS[0][1] * NXY, x_recv0)
    products(0, cut)
    send_group(0, send_y)
    spread_grads(0, cut)

    own_x.wait()
    arrived(NCHIP - 1 - GROUPS[0][1] * NXY, x_recv1)

    spread_grads(cut, NZ * SLOT)
    theirs, ours = 4 * (1 - core), 4 * core

    def weight_grads(k):
        both = lax.dot_general(xm[k], gall[...], (((0,), (0,)), ((), ())), preferred_element_type=F32)
        gwbuf[k, 0] = both[0:CH, :C] + both[CH:2 * CH, C:]
        gwbuf[k, 1] = both[0:CH, C:] - both[CH:2 * CH, :C]

    def exchange(k):
        return pltpu.make_async_remote_copy(
            src_ref=gwbuf.at[theirs + k], dst_ref=gwx.at[k], send_sem=e_send.at[k], recv_sem=e_recv.at[k],
            device_id={"blk": blk ^ 1, "chan": c}, device_id_type=MESH)

    for k in range(4):
        weight_grads(theirs + k)
        exchange(k).start()
    for k in range(4):
        weight_grads(ours + k)
    products(cut, NZ * SLOT)
    send_slots(send_y, 3, 5, 0)
    for k in range(4):
        exchange(k).wait_recv()
        gwbuf[ours + k] += gwx[k]
        mine = ours + k == c

        @pl.when(mine)
        def _():
            pltpu.make_async_copy(gwbuf.at[ours + k], gwr.at[c & 3], d_recv).start()

        @pl.when(jnp.logical_not(mine))
        def _():
            pltpu.make_async_remote_copy(
                src_ref=gwbuf.at[ours + k], dst_ref=gwr.at[c & 3], send_sem=d_send, recv_sem=d_recv,
                device_id={"blk": j * NC + (c >> 2), "chan": ours + k}, device_id_type=MESH).start()

    send_slots(send_y, 5, 8, 0)
    own_y = pltpu.make_async_copy(ybuf.at[c, own_rows], rbuf.at[j * NCH + c], y_loc)
    own_y.start()

    def done(buf, sem):
        pltpu.make_async_copy(buf, buf, sem).wait()

    @pl.when(w_self)
    def _():
        done(wrecv.at[pl.ds(0, 3)], w_send)
        hand_over.wait_send()
        done(gwr.at[pl.ds(0, 3)], d_send)

    @pl.when(jnp.logical_not(w_self))
    def _():
        done(wrecv.at[pl.ds(0, 4)], w_send)
        done(gwr, d_send)

    arrived(NCHIP - 1, x_send)
    arrived(NCHIP - 1, y_send)
    own_y.wait()
    for k in range(4):
        exchange(k).wait_send()
    done(gwr, d_recv)
    arrived(NCHIP - 1, y_recv)


def finish(rbuf, gwr, mask_ref, out_hbm, gin_hbm, gw_hbm, b32, xf, outv, ginv, gwv, s_out, s_gin, s_gw):
    for k in range(4):
        for p in range(2):
            gwv[k, p] = gwr[k, p] * mask_ref[k:k + 1, :]
    put_gw = pltpu.make_async_copy(gwv, gw_hbm, s_gw)
    put_gw.start()

    b32[...] = rbuf[...].astype(F32).reshape(2048, 128)
    for s in range(S):
        tile = b32[pl.ds(s, 128, stride=S), :].T
        for q in range(2):
            for p in range(2):
                row = (2 * q + p) * CH
                xf[pl.ds(q * 1024 + p * S + s, CH, stride=2 * S), :] = tile[row:row + CH]
    outv[...] = xf[0:1024, :].astype(BF16).reshape(CH, 2, S, 128)
    put_out = pltpu.make_async_copy(outv, out_hbm, s_out)
    put_out.start()
    ginv[...] = xf[1024:2048, :].astype(BF16).reshape(CH, 2, S, 128)
    put_gin = pltpu.make_async_copy(ginv, gin_hbm, s_gin)
    put_gin.start()
    put_gw.wait()
    put_out.wait()
    put_gin.wait()


def local(spec_in, weight, pattern, cotangent):
    vmem = pl.BlockSpec(memory_space=pltpu.VMEM)
    hbm = pl.BlockSpec(memory_space=pltpu.HBM)
    dma = pltpu.SemaphoreType.DMA
    tiles, sums, mask = pl.pallas_call(
        kernel,
        out_shape=(
            jax.ShapeDtypeStruct((NCHIP, S, 128), BF16),
            jax.ShapeDtypeStruct(weight.shape, F32),
            jax.ShapeDtypeStruct((4, C), F32),
        ),
        in_specs=[hbm, hbm, hbm, hbm],
        out_specs=(vmem, vmem, vmem),
        scratch_shapes=[
            pltpu.VMEM(spec_in.shape, BF16),
            pltpu.VMEM(spec_in.shape, BF16),
            pltpu.VMEM(weight.shape, BF16),
            pltpu.SMEM(pattern.shape, jnp.int32),
            pltpu.VMEM((2048, 128), F32),
            pltpu.VMEM((2048, 128), F32),
            pltpu.VMEM((NCHIP, S, 128), BF16),
            pltpu.VMEM((NCH, NZ * SLOT, 128), BF16),
            pltpu.VMEM((4, 2, CH, C), BF16),
            pltpu.VMEM((NCH, 2, CH, C), BF16),
            pltpu.VMEM((NCH * 128, NCH * 128), BF16),
            pltpu.VMEM((4, C, NCH * 128), BF16),
            pltpu.VMEM((NCH, NZ * SLOT, 128), BF16),
            pltpu.VMEM((NZ * SLOT, 2 * C), BF16),
            pltpu.VMEM((NCH, 2, CH, C), F32),
            pltpu.VMEM(weight.shape, F32),
            pltpu.SemaphoreType.REGULAR,
        ] + [dma] * 15 + [pltpu.SemaphoreType.DMA((4,))] * 2 + [dma] * 2,
        compiler_params=pltpu.CompilerParams(
            collective_id=0, has_side_effects=True, vmem_limit_bytes=40 << 20),
    )(*(pltpu.with_memory_space_constraint(a, pltpu.HBM) for a in (spec_in, weight, pattern, cotangent)))
    return pl.pallas_call(
        finish,
        out_shape=(
            jax.ShapeDtypeStruct(spec_in.shape, BF16),
            jax.ShapeDtypeStruct(spec_in.shape, BF16),
            jax.ShapeDtypeStruct(weight.shape, F32),
        ),
        in_specs=[vmem, vmem, vmem],
        out_specs=(hbm, hbm, hbm),
        scratch_shapes=[
            pltpu.VMEM((2048, 128), F32),
            pltpu.VMEM((2048, 128), F32),
            pltpu.VMEM(spec_in.shape, BF16),
            pltpu.VMEM(spec_in.shape, BF16),
            pltpu.VMEM(weight.shape, F32),
        ] + [dma] * 3,
        compiler_params=pltpu.CompilerParams(vmem_limit_bytes=16 << 20),
    )(tiles, sums, mask)


def solution(mesh):
    in_specs = (
        P("chan", None, "blk", None),
        P("blk", None, "chan", None),
        P("blk", None, None),
        P("chan", None, "blk", None),
    )
    out_specs = (
        P("chan", None, "blk", None),
        P("chan", None, "blk", None),
        P("blk", None, "chan", None),
    )
    return jax.shard_map(local, mesh=mesh, in_specs=in_specs, out_specs=out_specs, check_vma=False)
```

```python
import jax
import jax.numpy as jnp
from jax import lax
from jax.experimental import pallas as pl
from jax.experimental.pallas import tpu as pltpu
from jax.sharding import PartitionSpec as P

F32 = jnp.float32
BF16 = jnp.bfloat16
MESH = pl.DeviceIdType.MESH

NZ, NYL, NC, NYH, NX = 8, 2, 2, 2, 4
NJ = NZ * NYL
NCH = NYH * NX
NCHIP = NJ * NCH
NXY = NCHIP // NZ
CH = 32
S = 16
C = 256
PAD_M, PAD_O = 17, 33
SLOT = NYL * S

OFFSETS = (4, 3, 5, 2, 6, 1, 7, 0)
GROUPS = ((0, 3), (3, 8))


def kernel(x_hbm, w_hbm, pat_hbm, g_hbm, rbuf, gwr, mask_ref,
           xv, gv, wv, pat_ref, xf, b32, sbuf, xm, wmask, wrecv, wb, ebuf, ybuf, gall, gwbuf, gwx,
           known, in_x, in_g, in_w, in_p, x_send, x_recv0, x_recv1, x_loc,
           w_send, w_recv, h_send, h_recv, y_send, y_recv, y_loc, e_send, e_recv, d_send, d_recv):
    blk = lax.axis_index("blk")
    c = lax.axis_index("chan")
    core = blk & 1
    j = blk >> 1
    z = j >> 1
    y = (c >> 2) * NYL + (j & 1)
    x = c & 3
    x_recv = (x_recv0, x_recv1)

    fetch_x = pltpu.make_async_copy(x_hbm, xv, in_x)
    fetch_g = pltpu.make_async_copy(g_hbm, gv, in_g)
    fetch_w = pltpu.make_async_copy(w_hbm, wv, in_w)
    fetch_p = pltpu.make_async_copy(pat_hbm, pat_ref, in_p)
    fetch_p.start()
    fetch_w.start()
    fetch_x.start()
    fetch_g.start()

    barrier = pltpu.get_barrier_semaphore()

    def signal(sem, b, k):
        pl.semaphore_signal(sem, inc=1, device_id={"blk": b, "chan": k}, device_id_type=MESH)

    for t in range(1, NJ):
        signal(barrier, ((j ^ t) << 1) + core, c)
    for t in range(1, NCH):
        signal(barrier, blk, c ^ t)
    signal(barrier, blk ^ 1, c)

    lane = lax.broadcasted_iota(jnp.int32, (1, C), 1) // 64
    fetch_p.wait()
    fetch_w.wait()
    for k in range(4):
        row = jnp.zeros((1, C), F32)
        for b in range(4):
            row = jnp.where(lane == b, pat_ref[k, c >> 1, b].astype(F32), row)
        mask_ref[k:k + 1, :] = row
        for p in range(2):
            wmask[k, p] = (wv[k, p].astype(F32) * row).astype(BF16)

    pl.semaphore_wait(barrier, NJ - 1 + NCH - 1 + 1)
    for t in range(1, NCH):
        signal(known, blk, c ^ t)

    w_self = (c >> 2) == core
    for k in range(4):
        mine = 4 * core + k == c

        @pl.when(mine)
        def _():
            pltpu.make_async_copy(wmask.at[k], wrecv.at[c], w_recv).start()

        @pl.when(jnp.logical_not(mine))
        def _():
            pltpu.make_async_remote_copy(
                src_ref=wmask.at[k], dst_ref=wrecv.at[c], send_sem=w_send, recv_sem=w_recv,
                device_id={"blk": blk, "chan": 4 * core + k}, device_id_type=MESH).start()

    fetch_x.wait()
    fetch_g.wait()
    for q, buf in enumerate((xv, gv)):
        for i in range(CH):
            row = (q * CH + i) * PAD_O
            xf[row:row + 2 * S, :] = buf[i].reshape(2 * S, 128).astype(F32)
    for s in range(S):
        rows = [xf[pl.ds(q * CH * PAD_O + p * S + s, CH, stride=PAD_O), :] for q in range(2) for p in range(2)]
        b32[pl.ds(s, NCHIP, stride=PAD_M), :] = jnp.concatenate(rows, axis=0).T
    for m in range(NCHIP):
        sbuf[m] = b32[m * PAD_M:m * PAD_M + S, :].astype(BF16)

    def xy(u):
        ty = y ^ (u & 3)
        tx = (x + (u >> 2)) & 3
        return ty & 1, (ty >> 1) * NX + tx

    def rows_of(slot, yl):
        return pl.ds(pl.multiple_of(slot * SLOT + yl * S, S), S)

    own_rows = rows_of(NZ - 1, j & 1)

    def send_x(g, slot, u):
        yl, tc = xy(u)
        tj = ((z + OFFSETS[slot]) & 7) * NYL + yl
        pltpu.make_async_remote_copy(
            src_ref=sbuf.at[tj * NCH + tc], dst_ref=xm.at[c, rows_of(slot, j & 1)],
            send_sem=x_send, recv_sem=x_recv[g],
            device_id={"blk": tj * NC + core, "chan": tc}, device_id_type=MESH).start()

    def send_y(slot, u):
        yl, tc = xy(u)
        tj = ((z - OFFSETS[slot]) & 7) * NYL + yl
        pltpu.make_async_remote_copy(
            src_ref=ybuf.at[tc, rows_of(slot, yl)], dst_ref=rbuf.at[j * NCH + c],
            send_sem=y_send, recv_sem=y_recv,
            device_id={"blk": tj * NC + core, "chan": tc}, device_id_type=MESH).start()

    def send_slots(send, first, last, start, also=None):
        def step(u, carry):
            for slot in range(first, min(last, NZ - 1)):
                send(slot, u)
            if also is not None:
                also(u)
            return carry

        lax.fori_loop(start, NXY, step, 0)
        if last == NZ:
            def plane(u, carry):
                send(NZ - 1, u)
                return carry

            lax.fori_loop(max(start, 1), NXY, plane, 0)

    def send_group(g, send, start=0):
        send_slots(send, *GROUPS[g], start)

    for u in range(2):
        for g, (first, last) in enumerate(GROUPS):
            for slot in range(first, last - 1 if last == NZ and u == 0 else last):
                send_x(g, slot, u)
    pl.semaphore_wait(known, NCH - 1)
    send_group(0, lambda slot, u: send_x(0, slot, u), 2)
    send_group(1, lambda slot, u: send_x(1, slot, u), 2)
    own_x = pltpu.make_async_copy(sbuf.at[j * NCH + c], xm.at[c, own_rows], x_loc)
    own_x.start()

    for q in range(4):
        o = lax.broadcasted_iota(jnp.int32, (C, NCH * 128), 0)
        l = lax.broadcasted_iota(jnp.int32, (C, NCH * 128), 1)
        ebuf[q] = (l == (o // CH) * 128 + q * CH + o % CH).astype(F32).astype(BF16)

    hand_over = pltpu.make_async_remote_copy(
        src_ref=wrecv, dst_ref=wrecv, send_sem=h_send, recv_sem=h_recv,
        device_id={"blk": blk ^ 1, "chan": c}, device_id_type=MESH)

    @pl.when(w_self)
    def _():
        pltpu.make_async_copy(wrecv, wrecv, w_recv).wait()
        hand_over.start()

    @pl.when(jnp.logical_not(w_self))
    def _():
        hand_over.wait_recv()

    wr = wrecv[:, 0].reshape(C, C)
    wi = wrecv[:, 1].reshape(C, C)
    wrt = wr.astype(F32).T.astype(BF16)
    wit = wi.astype(F32).T.astype(BF16)

    def spread(a, qa, b, qb):
        left = jnp.dot(a, ebuf[qa], preferred_element_type=F32)
        return (left + jnp.dot(b, ebuf[qb], preferred_element_type=F32)).astype(BF16)

    for part, rows in enumerate((spread(wr, 0, wi, 1), spread(-wi, 0, wr, 1),
                                 spread(wrt, 2, -wit, 3), spread(wit, 2, wrt, 3))):
        for k in range(NCH):
            wb[k * 128 + part * CH:k * 128 + part * CH + CH, :] = rows[k * CH:(k + 1) * CH, :]

    def load(lo, hi):
        return jnp.concatenate([xm[k, lo:hi] for k in range(NCH)], axis=1)

    def spread_grads(lo, hi):
        for h in range(2):
            gall[lo:hi, h * C:(h + 1) * C] = lax.dot_general(
                load(lo, hi), ebuf[2 + h], (((1,), (1,)), ((), ())), preferred_element_type=F32).astype(BF16)

    def products(lo, hi):
        rows = load(lo, hi)
        for n in range(4):
            part = jnp.dot(rows, wb[:, n * 256:(n + 1) * 256], preferred_element_type=F32).astype(BF16)
            ybuf[2 * n, lo:hi] = part[:, :128]
            ybuf[2 * n + 1, lo:hi] = part[:, 128:]

    cut = GROUPS[0][1] * SLOT

    def arrived(n, sem):
        pltpu.make_async_copy(sbuf.at[pl.ds(0, n)], sbuf.at[pl.ds(0, n)], sem).wait()

    arrived(GROUPS[0][1] * NXY, x_recv0)
    products(0, cut)
    send_group(0, send_y)
    spread_grads(0, cut)

    own_x.wait()
    arrived(NCHIP - 1 - GROUPS[0][1] * NXY, x_recv1)

    spread_grads(cut, NZ * SLOT)
    theirs, ours = 4 * (1 - core), 4 * core

    def weight_grads(k):
        both = lax.dot_general(xm[k], gall[...], (((0,), (0,)), ((), ())), preferred_element_type=F32)
        gwbuf[k, 0] = both[0:CH, :C] + both[CH:2 * CH, C:]
        gwbuf[k, 1] = both[0:CH, C:] - both[CH:2 * CH, :C]

    def exchange(k):
        return pltpu.make_async_remote_copy(
            src_ref=gwbuf.at[theirs + k], dst_ref=gwx.at[k], send_sem=e_send.at[k], recv_sem=e_recv.at[k],
            device_id={"blk": blk ^ 1, "chan": c}, device_id_type=MESH)

    for k in range(4):
        weight_grads(theirs + k)
        exchange(k).start()
    for k in range(4):
        weight_grads(ours + k)
    products(cut, NZ * SLOT)
    send_slots(send_y, 3, 5, 0)
    for k in range(4):
        exchange(k).wait_recv()
        gwbuf[ours + k] += gwx[k]
        mine = ours + k == c

        @pl.when(mine)
        def _():
            pltpu.make_async_copy(gwbuf.at[ours + k], gwr.at[c & 3], d_recv).start()

        @pl.when(jnp.logical_not(mine))
        def _():
            pltpu.make_async_remote_copy(
                src_ref=gwbuf.at[ours + k], dst_ref=gwr.at[c & 3], send_sem=d_send, recv_sem=d_recv,
                device_id={"blk": j * NC + (c >> 2), "chan": ours + k}, device_id_type=MESH).start()

    send_slots(send_y, 5, 8, 0)
    own_y = pltpu.make_async_copy(ybuf.at[c, own_rows], rbuf.at[j * NCH + c], y_loc)
    own_y.start()

    def done(buf, sem):
        pltpu.make_async_copy(buf, buf, sem).wait()

    @pl.when(w_self)
    def _():
        done(wrecv.at[pl.ds(0, 3)], w_send)
        hand_over.wait_send()
        done(gwr.at[pl.ds(0, 3)], d_send)

    @pl.when(jnp.logical_not(w_self))
    def _():
        done(wrecv.at[pl.ds(0, 4)], w_send)
        done(gwr, d_send)

    arrived(NCHIP - 1, x_send)
    arrived(NCHIP - 1, y_send)
    own_y.wait()
    for k in range(4):
        exchange(k).wait_send()
    done(gwr, d_recv)
    arrived(NCHIP - 1, y_recv)


def finish(rbuf, gwr, mask_ref, out_hbm, gin_hbm, gw_hbm, b32, xf, outv, ginv, gwv, s_out, s_gin, s_gw):
    for k in range(4):
        for p in range(2):
            gwv[k, p] = gwr[k, p] * mask_ref[k:k + 1, :]
    put_gw = pltpu.make_async_copy(gwv, gw_hbm, s_gw)
    put_gw.start()

    for m in range(NCHIP):
        b32[m * PAD_M:m * PAD_M + S, :] = rbuf[m].astype(F32)
    for s in range(S):
        tile = b32[pl.ds(s, NCHIP, stride=PAD_M), :].T
        for q in range(2):
            for p in range(2):
                row = (2 * q + p) * CH
                xf[pl.ds(q * CH * PAD_O + p * S + s, CH, stride=PAD_O), :] = tile[row:row + CH]
    for q, buf in enumerate((outv, ginv)):
        for o in range(CH):
            row = (q * CH + o) * PAD_O
            buf[o] = xf[row:row + 2 * S, :].astype(BF16).reshape(2, S, 128)
        if q == 0:
            put_out = pltpu.make_async_copy(outv, out_hbm, s_out)
            put_out.start()
    put_gin = pltpu.make_async_copy(ginv, gin_hbm, s_gin)
    put_gin.start()
    put_gw.wait()
    put_out.wait()
    put_gin.wait()


def local(spec_in, weight, pattern, cotangent):
    vmem = pl.BlockSpec(memory_space=pltpu.VMEM)
    hbm = pl.BlockSpec(memory_space=pltpu.HBM)
    dma = pltpu.SemaphoreType.DMA
    tiles, sums, mask = pl.pallas_call(
        kernel,
        out_shape=(
            jax.ShapeDtypeStruct((NCHIP, S, 128), BF16),
            jax.ShapeDtypeStruct(weight.shape, F32),
            jax.ShapeDtypeStruct((4, C), F32),
        ),
        in_specs=[hbm, hbm, hbm, hbm],
        out_specs=(vmem, vmem, vmem),
        scratch_shapes=[
            pltpu.VMEM(spec_in.shape, BF16),
            pltpu.VMEM(spec_in.shape, BF16),
            pltpu.VMEM(weight.shape, BF16),
            pltpu.SMEM(pattern.shape, jnp.int32),
            pltpu.VMEM((2 * CH * PAD_O, 128), F32),
            pltpu.VMEM((NCHIP * PAD_M, 128), F32),
            pltpu.VMEM((NCHIP, S, 128), BF16),
            pltpu.VMEM((NCH, NZ * SLOT, 128), BF16),
            pltpu.VMEM((4, 2, CH, C), BF16),
            pltpu.VMEM((NCH, 2, CH, C), BF16),
            pltpu.VMEM((NCH * 128, NCH * 128), BF16),
            pltpu.VMEM((4, C, NCH * 128), BF16),
            pltpu.VMEM((NCH, NZ * SLOT, 128), BF16),
            pltpu.VMEM((NZ * SLOT, 2 * C), BF16),
            pltpu.VMEM((NCH, 2, CH, C), F32),
            pltpu.VMEM(weight.shape, F32),
            pltpu.SemaphoreType.REGULAR,
        ] + [dma] * 15 + [pltpu.SemaphoreType.DMA((4,))] * 2 + [dma] * 2,
        compiler_params=pltpu.CompilerParams(
            collective_id=0, has_side_effects=True, vmem_limit_bytes=40 << 20),
    )(*(pltpu.with_memory_space_constraint(a, pltpu.HBM) for a in (spec_in, weight, pattern, cotangent)))
    return pl.pallas_call(
        finish,
        out_shape=(
            jax.ShapeDtypeStruct(spec_in.shape, BF16),
            jax.ShapeDtypeStruct(spec_in.shape, BF16),
            jax.ShapeDtypeStruct(weight.shape, F32),
        ),
        in_specs=[vmem, vmem, vmem],
        out_specs=(hbm, hbm, hbm),
        scratch_shapes=[
            pltpu.VMEM((NCHIP * PAD_M, 128), F32),
            pltpu.VMEM((2 * CH * PAD_O, 128), F32),
            pltpu.VMEM(spec_in.shape, BF16),
            pltpu.VMEM(spec_in.shape, BF16),
            pltpu.VMEM(weight.shape, F32),
        ] + [dma] * 3,
        compiler_params=pltpu.CompilerParams(vmem_limit_bytes=16 << 20),
    )(tiles, sums, mask)


def solution(mesh):
    in_specs = (
        P("chan", None, "blk", None),
        P("blk", None, "chan", None),
        P("blk", None, None),
        P("chan", None, "blk", None),
    )
    out_specs = (
        P("chan", None, "blk", None),
        P("chan", None, "blk", None),
        P("blk", None, "chan", None),
    )
    return jax.shard_map(local, mesh=mesh, in_specs=in_specs, out_specs=out_specs, check_vma=False)
```

```python
import jax
import jax.numpy as jnp
from jax import lax
from jax.experimental import pallas as pl
from jax.experimental.pallas import tpu as pltpu
from jax.sharding import PartitionSpec as P

F32 = jnp.float32
BF16 = jnp.bfloat16
MESH = pl.DeviceIdType.MESH

NZ, NYL, NC, NYH, NX = 8, 2, 2, 2, 4
NJ = NZ * NYL
NCH = NYH * NX
NCHIP = NJ * NCH
NXY = NCHIP // NZ
CH = 32
S = 16
C = 256
PAD_M, PAD_O = 17, 33
SLOT = NYL * S

OFFSETS = (4, 3, 5, 2, 6, 1, 7, 0)
GROUPS = ((0, 3), (3, 8))


def kernel(x_hbm, w_hbm, pat_hbm, g_hbm, rbuf, gwr, mask_ref,
           xv, gv, wv, pat_ref, xf, b32, sbuf, xm, wmask, wrecv, wb, ebuf, ybuf, gall, gwbuf, gwx,
           known, in_x, in_g, in_w, in_p, x_send, x_recv0, x_recv1, x_loc,
           w_send, w_recv, h_send, h_recv, y_send, y_recv, y_loc, e_send, e_recv, d_send, d_recv):
    blk = lax.axis_index("blk")
    c = lax.axis_index("chan")
    core = blk & 1
    j = blk >> 1
    z = j >> 1
    y = (c >> 2) * NYL + (j & 1)
    x = c & 3
    x_recv = (x_recv0, x_recv1)

    fetch_x = pltpu.make_async_copy(x_hbm, xv, in_x)
    fetch_g = pltpu.make_async_copy(g_hbm, gv, in_g)
    fetch_w = pltpu.make_async_copy(w_hbm, wv, in_w)
    fetch_p = pltpu.make_async_copy(pat_hbm, pat_ref, in_p)
    fetch_p.start()
    fetch_w.start()
    fetch_x.start()
    fetch_g.start()

    barrier = pltpu.get_barrier_semaphore()

    def signal(sem, b, k):
        pl.semaphore_signal(sem, inc=1, device_id={"blk": b, "chan": k}, device_id_type=MESH)

    for t in range(1, NJ):
        signal(barrier, ((j ^ t) << 1) + core, c)
    for t in range(1, NCH):
        signal(barrier, blk, c ^ t)
    signal(barrier, blk ^ 1, c)

    lane = lax.broadcasted_iota(jnp.int32, (1, C), 1) // 64
    fetch_p.wait()
    fetch_w.wait()
    for k in range(4):
        row = jnp.zeros((1, C), F32)
        for b in range(4):
            row = jnp.where(lane == b, pat_ref[k, c >> 1, b].astype(F32), row)
        mask_ref[k:k + 1, :] = row
        for p in range(2):
            wmask[k, p] = (wv[k, p].astype(F32) * row).astype(BF16)

    pl.semaphore_wait(barrier, NJ - 1 + NCH - 1 + 1)
    for t in range(1, NCH):
        signal(known, blk, c ^ t)

    w_self = (c >> 2) == core
    for k in range(4):
        mine = 4 * core + k == c

        @pl.when(mine)
        def _():
            pltpu.make_async_copy(wmask.at[k], wrecv.at[c], w_recv).start()

        @pl.when(jnp.logical_not(mine))
        def _():
            pltpu.make_async_remote_copy(
                src_ref=wmask.at[k], dst_ref=wrecv.at[c], send_sem=w_send, recv_sem=w_recv,
                device_id={"blk": blk, "chan": 4 * core + k}, device_id_type=MESH).start()

    fetch_x.wait()
    fetch_g.wait()
    xf[0:1024, :] = xv[...].reshape(1024, 128).astype(F32)
    xf[1024:2048, :] = gv[...].reshape(1024, 128).astype(F32)
    for s in range(S):
        rows = [xf[pl.ds(q * 1024 + p * S + s, CH, stride=2 * S), :] for q in range(2) for p in range(2)]
        b32[pl.ds(s, 128, stride=S), :] = jnp.concatenate(rows, axis=0).T
    sbuf[...] = b32[...].reshape(128, S, 128).astype(BF16)

    def xy(u):
        ty = y ^ (u & 3)
        tx = (x + (u >> 2)) & 3
        return ty & 1, (ty >> 1) * NX + tx

    def rows_of(slot, yl):
        return pl.ds(pl.multiple_of(slot * SLOT + yl * S, S), S)

    own_rows = rows_of(NZ - 1, j & 1)

    def send_x(g, slot, u):
        yl, tc = xy(u)
        tj = ((z + OFFSETS[slot]) & 7) * NYL + yl
        pltpu.make_async_remote_copy(
            src_ref=sbuf.at[tj * NCH + tc], dst_ref=xm.at[c, rows_of(slot, j & 1)],
            send_sem=x_send, recv_sem=x_recv[g],
            device_id={"blk": tj * NC + core, "chan": tc}, device_id_type=MESH).start()

    def send_y(slot, u):
        yl, tc = xy(u)
        tj = ((z - OFFSETS[slot]) & 7) * NYL + yl
        pltpu.make_async_remote_copy(
            src_ref=ybuf.at[tc, rows_of(slot, yl)], dst_ref=rbuf.at[j * NCH + c],
            send_sem=y_send, recv_sem=y_recv,
            device_id={"blk": tj * NC + core, "chan": tc}, device_id_type=MESH).start()

    def send_slots(send, first, last, start, also=None):
        def step(u, carry):
            for slot in range(first, min(last, NZ - 1)):
                send(slot, u)
            if also is not None:
                also(u)
            return carry

        lax.fori_loop(start, NXY, step, 0)
        if last == NZ:
            def plane(u, carry):
                send(NZ - 1, u)
                return carry

            lax.fori_loop(max(start, 1), NXY, plane, 0)

    def send_group(g, send, start=0):
        send_slots(send, *GROUPS[g], start)

    for u in range(2):
        for g, (first, last) in enumerate(GROUPS):
            for slot in range(first, last - 1 if last == NZ and u == 0 else last):
                send_x(g, slot, u)
    pl.semaphore_wait(known, NCH - 1)
    send_group(0, lambda slot, u: send_x(0, slot, u), 2)
    send_group(1, lambda slot, u: send_x(1, slot, u), 2)
    own_x = pltpu.make_async_copy(sbuf.at[j * NCH + c], xm.at[c, own_rows], x_loc)
    own_x.start()

    for q in range(4):
        o = lax.broadcasted_iota(jnp.int32, (C, NCH * 128), 0)
        l = lax.broadcasted_iota(jnp.int32, (C, NCH * 128), 1)
        ebuf[q] = (l == (o // CH) * 128 + q * CH + o % CH).astype(F32).astype(BF16)

    hand_over = pltpu.make_async_remote_copy(
        src_ref=wrecv, dst_ref=wrecv, send_sem=h_send, recv_sem=h_recv,
        device_id={"blk": blk ^ 1, "chan": c}, device_id_type=MESH)

    @pl.when(w_self)
    def _():
        pltpu.make_async_copy(wrecv, wrecv, w_recv).wait()
        hand_over.start()

    @pl.when(jnp.logical_not(w_self))
    def _():
        hand_over.wait_recv()

    wr = wrecv[:, 0].reshape(C, C)
    wi = wrecv[:, 1].reshape(C, C)
    wrt = wr.astype(F32).T.astype(BF16)
    wit = wi.astype(F32).T.astype(BF16)

    def spread(a, qa, b, qb):
        left = jnp.dot(a, ebuf[qa], preferred_element_type=F32)
        return (left + jnp.dot(b, ebuf[qb], preferred_element_type=F32)).astype(BF16)

    for part, rows in enumerate((spread(wr, 0, wi, 1), spread(-wi, 0, wr, 1),
                                 spread(wrt, 2, -wit, 3), spread(wit, 2, wrt, 3))):
        for k in range(NCH):
            wb[k * 128 + part * CH:k * 128 + part * CH + CH, :] = rows[k * CH:(k + 1) * CH, :]

    def load(lo, hi):
        return jnp.concatenate([xm[k, lo:hi] for k in range(NCH)], axis=1)

    def spread_grads(lo, hi):
        for h in range(2):
            gall[lo:hi, h * C:(h + 1) * C] = lax.dot_general(
                load(lo, hi), ebuf[2 + h], (((1,), (1,)), ((), ())), preferred_element_type=F32).astype(BF16)

    def products(lo, hi):
        rows = load(lo, hi)
        for n in range(4):
            part = jnp.dot(rows, wb[:, n * 256:(n + 1) * 256], preferred_element_type=F32).astype(BF16)
            ybuf[2 * n, lo:hi] = part[:, :128]
            ybuf[2 * n + 1, lo:hi] = part[:, 128:]

    cut = GROUPS[0][1] * SLOT

    def arrived(n, sem):
        pltpu.make_async_copy(sbuf.at[pl.ds(0, n)], sbuf.at[pl.ds(0, n)], sem).wait()

    arrived(GROUPS[0][1] * NXY, x_recv0)
    products(0, cut)
    send_group(0, send_y)
    spread_grads(0, cut)

    own_x.wait()
    arrived(NCHIP - 1 - GROUPS[0][1] * NXY, x_recv1)

    spread_grads(cut, NZ * SLOT)
    theirs, ours = 4 * (1 - core), 4 * core

    def weight_grads(k):
        both = lax.dot_general(xm[k], gall[...], (((0,), (0,)), ((), ())), preferred_element_type=F32)
        gwbuf[k, 0] = both[0:CH, :C] + both[CH:2 * CH, C:]
        gwbuf[k, 1] = both[0:CH, C:] - both[CH:2 * CH, :C]

    def exchange(k):
        return pltpu.make_async_remote_copy(
            src_ref=gwbuf.at[theirs + k], dst_ref=gwx.at[k], send_sem=e_send.at[k], recv_sem=e_recv.at[k],
            device_id={"blk": blk ^ 1, "chan": c}, device_id_type=MESH)

    for k in range(4):
        weight_grads(theirs + k)
        exchange(k).start()
    for k in range(4):
        weight_grads(ours + k)
    products(cut, NZ * SLOT)
    send_slots(send_y, 3, 5, 0)
    for k in range(4):
        exchange(k).wait_recv()
        gwbuf[ours + k] += gwx[k]
        mine = ours + k == c

        @pl.when(mine)
        def _():
            pltpu.make_async_copy(gwbuf.at[ours + k], gwr.at[c & 3], d_recv).start()

        @pl.when(jnp.logical_not(mine))
        def _():
            pltpu.make_async_remote_copy(
                src_ref=gwbuf.at[ours + k], dst_ref=gwr.at[c & 3], send_sem=d_send, recv_sem=d_recv,
                device_id={"blk": j * NC + (c >> 2), "chan": ours + k}, device_id_type=MESH).start()

    send_slots(send_y, 5, 8, 0)
    own_y = pltpu.make_async_copy(ybuf.at[c, own_rows], rbuf.at[j * NCH + c], y_loc)
    own_y.start()

    def done(buf, sem):
        pltpu.make_async_copy(buf, buf, sem).wait()

    @pl.when(w_self)
    def _():
        done(wrecv.at[pl.ds(0, 3)], w_send)
        hand_over.wait_send()
        done(gwr.at[pl.ds(0, 3)], d_send)

    @pl.when(jnp.logical_not(w_self))
    def _():
        done(wrecv.at[pl.ds(0, 4)], w_send)
        done(gwr, d_send)

    arrived(NCHIP - 1, x_send)
    arrived(NCHIP - 1, y_send)
    own_y.wait()
    for k in range(4):
        exchange(k).wait_send()
    done(gwr, d_recv)
    arrived(NCHIP - 1, y_recv)


def finish(rbuf, gwr, mask_ref, out_hbm, gin_hbm, gw_hbm, b32, xf, outv, ginv, gwv, s_out, s_gin, s_gw):
    for k in range(4):
        for p in range(2):
            gwv[k, p] = gwr[k, p] * mask_ref[k:k + 1, :]
    put_gw = pltpu.make_async_copy(gwv, gw_hbm, s_gw)
    put_gw.start()

    for m in range(NCHIP):
        b32[m * PAD_M:m * PAD_M + S, :] = rbuf[m].astype(F32)
    for s in range(S):
        tile = b32[pl.ds(s, NCHIP, stride=PAD_M), :].T
        for q in range(2):
            for p in range(2):
                row = (2 * q + p) * CH
                xf[pl.ds(q * CH * PAD_O + p * S + s, CH, stride=PAD_O), :] = tile[row:row + CH]
    for q, buf in enumerate((outv, ginv)):
        for o in range(CH):
            row = (q * CH + o) * PAD_O
            buf[o] = xf[row:row + 2 * S, :].astype(BF16).reshape(2, S, 128)
        if q == 0:
            put_out = pltpu.make_async_copy(outv, out_hbm, s_out)
            put_out.start()
    put_gin = pltpu.make_async_copy(ginv, gin_hbm, s_gin)
    put_gin.start()
    put_gw.wait()
    put_out.wait()
    put_gin.wait()


def local(spec_in, weight, pattern, cotangent):
    vmem = pl.BlockSpec(memory_space=pltpu.VMEM)
    hbm = pl.BlockSpec(memory_space=pltpu.HBM)
    dma = pltpu.SemaphoreType.DMA
    tiles, sums, mask = pl.pallas_call(
        kernel,
        out_shape=(
            jax.ShapeDtypeStruct((NCHIP, S, 128), BF16),
            jax.ShapeDtypeStruct(weight.shape, F32),
            jax.ShapeDtypeStruct((4, C), F32),
        ),
        in_specs=[hbm, hbm, hbm, hbm],
        out_specs=(vmem, vmem, vmem),
        scratch_shapes=[
            pltpu.VMEM(spec_in.shape, BF16),
            pltpu.VMEM(spec_in.shape, BF16),
            pltpu.VMEM(weight.shape, BF16),
            pltpu.SMEM(pattern.shape, jnp.int32),
            pltpu.VMEM((2048, 128), F32),
            pltpu.VMEM((2048, 128), F32),
            pltpu.VMEM((NCHIP, S, 128), BF16),
            pltpu.VMEM((NCH, NZ * SLOT, 128), BF16),
            pltpu.VMEM((4, 2, CH, C), BF16),
            pltpu.VMEM((NCH, 2, CH, C), BF16),
            pltpu.VMEM((NCH * 128, NCH * 128), BF16),
            pltpu.VMEM((4, C, NCH * 128), BF16),
            pltpu.VMEM((NCH, NZ * SLOT, 128), BF16),
            pltpu.VMEM((NZ * SLOT, 2 * C), BF16),
            pltpu.VMEM((NCH, 2, CH, C), F32),
            pltpu.VMEM(weight.shape, F32),
            pltpu.SemaphoreType.REGULAR,
        ] + [dma] * 15 + [pltpu.SemaphoreType.DMA((4,))] * 2 + [dma] * 2,
        compiler_params=pltpu.CompilerParams(
            collective_id=0, has_side_effects=True, vmem_limit_bytes=40 << 20),
    )(*(pltpu.with_memory_space_constraint(a, pltpu.HBM) for a in (spec_in, weight, pattern, cotangent)))
    return pl.pallas_call(
        finish,
        out_shape=(
            jax.ShapeDtypeStruct(spec_in.shape, BF16),
            jax.ShapeDtypeStruct(spec_in.shape, BF16),
            jax.ShapeDtypeStruct(weight.shape, F32),
        ),
        in_specs=[vmem, vmem, vmem],
        out_specs=(hbm, hbm, hbm),
        scratch_shapes=[
            pltpu.VMEM((NCHIP * PAD_M, 128), F32),
            pltpu.VMEM((2 * CH * PAD_O, 128), F32),
            pltpu.VMEM(spec_in.shape, BF16),
            pltpu.VMEM(spec_in.shape, BF16),
            pltpu.VMEM(weight.shape, F32),
        ] + [dma] * 3,
        compiler_params=pltpu.CompilerParams(vmem_limit_bytes=16 << 20),
    )(tiles, sums, mask)


def solution(mesh):
    in_specs = (
        P("chan", None, "blk", None),
        P("blk", None, "chan", None),
        P("blk", None, None),
        P("chan", None, "blk", None),
    )
    out_specs = (
        P("chan", None, "blk", None),
        P("chan", None, "blk", None),
        P("blk", None, "chan", None),
    )
    return jax.shard_map(local, mesh=mesh, in_specs=in_specs, out_specs=out_specs, check_vma=False)
```

```python
import jax
import jax.numpy as jnp
from jax import lax
from jax.experimental import pallas as pl
from jax.experimental.pallas import tpu as pltpu
from jax.sharding import PartitionSpec as P

F32 = jnp.float32
BF16 = jnp.bfloat16
MESH = pl.DeviceIdType.MESH

NZ, NYL, NC, NYH, NX = 8, 2, 2, 2, 4
NJ = NZ * NYL
NCH = NYH * NX
NCHIP = NJ * NCH
NXY = NCHIP // NZ
CH = 32
S = 16
C = 256
PAD_M, PAD_O = 17, 33
SLOT = NYL * S

OFFSETS = (4, 3, 5, 2, 6, 1, 7, 0)
TURNS = (0, 4, 8, 12, 2, 6, 10, 0)
GROUPS = ((0, 3), (3, 8))


def kernel(x_hbm, w_hbm, pat_hbm, g_hbm, rbuf, gwr, mask_ref,
           xv, gv, wv, pat_ref, xf, b32, sbuf, xm, wmask, wrecv, wb, ebuf, ybuf, gall, gwbuf, gwx,
           known, in_x, in_g, in_w, in_p, x_send, x_recv0, x_recv1, x_loc,
           w_send, w_recv, h_send, h_recv, y_send, y_recv, y_loc, e_send, e_recv, d_send, d_recv):
    blk = lax.axis_index("blk")
    c = lax.axis_index("chan")
    core = blk & 1
    j = blk >> 1
    z = j >> 1
    y = (c >> 2) * NYL + (j & 1)
    x = c & 3
    x_recv = (x_recv0, x_recv1)

    fetch_x = pltpu.make_async_copy(x_hbm, xv, in_x)
    fetch_g = pltpu.make_async_copy(g_hbm, gv, in_g)
    fetch_w = pltpu.make_async_copy(w_hbm, wv, in_w)
    fetch_p = pltpu.make_async_copy(pat_hbm, pat_ref, in_p)
    fetch_p.start()
    fetch_w.start()
    fetch_x.start()
    fetch_g.start()

    barrier = pltpu.get_barrier_semaphore()

    def signal(sem, b, k):
        pl.semaphore_signal(sem, inc=1, device_id={"blk": b, "chan": k}, device_id_type=MESH)

    for t in range(1, NJ):
        signal(barrier, ((j ^ t) << 1) + core, c)
    for t in range(1, NCH):
        signal(barrier, blk, c ^ t)
    signal(barrier, blk ^ 1, c)

    lane = lax.broadcasted_iota(jnp.int32, (1, C), 1) // 64
    fetch_p.wait()
    fetch_w.wait()
    for k in range(4):
        row = jnp.zeros((1, C), F32)
        for b in range(4):
            row = jnp.where(lane == b, pat_ref[k, c >> 1, b].astype(F32), row)
        mask_ref[k:k + 1, :] = row
        for p in range(2):
            wmask[k, p] = (wv[k, p].astype(F32) * row).astype(BF16)

    pl.semaphore_wait(barrier, NJ - 1 + NCH - 1 + 1)
    for t in range(1, NCH):
        signal(known, blk, c ^ t)

    w_self = (c >> 2) == core
    for k in range(4):
        mine = 4 * core + k == c

        @pl.when(mine)
        def _():
            pltpu.make_async_copy(wmask.at[k], wrecv.at[c], w_recv).start()

        @pl.when(jnp.logical_not(mine))
        def _():
            pltpu.make_async_remote_copy(
                src_ref=wmask.at[k], dst_ref=wrecv.at[c], send_sem=w_send, recv_sem=w_recv,
                device_id={"blk": blk, "chan": 4 * core + k}, device_id_type=MESH).start()

    fetch_x.wait()
    fetch_g.wait()
    xf[0:1024, :] = xv[...].reshape(1024, 128).astype(F32)
    xf[1024:2048, :] = gv[...].reshape(1024, 128).astype(F32)
    for s in range(S):
        rows = [xf[pl.ds(q * 1024 + p * S + s, CH, stride=2 * S), :] for q in range(2) for p in range(2)]
        b32[pl.ds(s, 128, stride=S), :] = jnp.concatenate(rows, axis=0).T
    sbuf[...] = b32[...].reshape(128, S, 128).astype(BF16)

    def xy(u):
        ty = y ^ (u & 3)
        tx = (x + (u >> 2)) & 3
        return ty & 1, (ty >> 1) * NX + tx

    def rows_of(slot, yl):
        return pl.ds(pl.multiple_of(slot * SLOT + yl * S, S), S)

    own_rows = rows_of(NZ - 1, j & 1)

    def send_x(g, slot, u):
        yl, tc = xy(u)
        tj = ((z + OFFSETS[slot]) & 7) * NYL + yl
        pltpu.make_async_remote_copy(
            src_ref=sbuf.at[tj * NCH + tc], dst_ref=xm.at[c, rows_of(slot, j & 1)],
            send_sem=x_send, recv_sem=x_recv[g],
            device_id={"blk": tj * NC + core, "chan": tc}, device_id_type=MESH).start()

    def send_y(slot, u):
        yl, tc = xy(u)
        tj = ((z - OFFSETS[slot]) & 7) * NYL + yl
        pltpu.make_async_remote_copy(
            src_ref=ybuf.at[tc, rows_of(slot, yl)], dst_ref=rbuf.at[j * NCH + c],
            send_sem=y_send, recv_sem=y_recv,
            device_id={"blk": tj * NC + core, "chan": tc}, device_id_type=MESH).start()

    def turned(u, by, start):
        v = u - start + by
        return start + jnp.where(v >= NXY - start, v - (NXY - start), v)

    def send_slots(send, first, last, start, also=None):
        def step(u, carry):
            for slot in range(first, min(last, NZ - 1)):
                send(slot, turned(u, TURNS[slot], start))
            if also is not None:
                also(u)
            return carry

        lax.fori_loop(start, NXY, step, 0)
        if last == NZ:
            def plane(u, carry):
                send(NZ - 1, u)
                return carry

            lax.fori_loop(max(start, 1), NXY, plane, 0)

    def send_group(g, send, start=0):
        send_slots(send, *GROUPS[g], start)

    for u in range(2):
        for g, (first, last) in enumerate(GROUPS):
            for slot in range(first, last - 1 if last == NZ and u == 0 else last):
                send_x(g, slot, u)
    pl.semaphore_wait(known, NCH - 1)
    send_group(0, lambda slot, u: send_x(0, slot, u), 2)
    send_group(1, lambda slot, u: send_x(1, slot, u), 2)
    own_x = pltpu.make_async_copy(sbuf.at[j * NCH + c], xm.at[c, own_rows], x_loc)
    own_x.start()

    for q in range(4):
        o = lax.broadcasted_iota(jnp.int32, (C, NCH * 128), 0)
        l = lax.broadcasted_iota(jnp.int32, (C, NCH * 128), 1)
        ebuf[q] = (l == (o // CH) * 128 + q * CH + o % CH).astype(F32).astype(BF16)

    hand_over = pltpu.make_async_remote_copy(
        src_ref=wrecv, dst_ref=wrecv, send_sem=h_send, recv_sem=h_recv,
        device_id={"blk": blk ^ 1, "chan": c}, device_id_type=MESH)

    @pl.when(w_self)
    def _():
        pltpu.make_async_copy(wrecv, wrecv, w_recv).wait()
        hand_over.start()

    @pl.when(jnp.logical_not(w_self))
    def _():
        hand_over.wait_recv()

    wr = wrecv[:, 0].reshape(C, C)
    wi = wrecv[:, 1].reshape(C, C)
    wrt = wr.astype(F32).T.astype(BF16)
    wit = wi.astype(F32).T.astype(BF16)

    def spread(a, qa, b, qb):
        left = jnp.dot(a, ebuf[qa], preferred_element_type=F32)
        return (left + jnp.dot(b, ebuf[qb], preferred_element_type=F32)).astype(BF16)

    for part, rows in enumerate((spread(wr, 0, wi, 1), spread(-wi, 0, wr, 1),
                                 spread(wrt, 2, -wit, 3), spread(wit, 2, wrt, 3))):
        for k in range(NCH):
            wb[k * 128 + part * CH:k * 128 + part * CH + CH, :] = rows[k * CH:(k + 1) * CH, :]

    def load(lo, hi):
        return jnp.concatenate([xm[k, lo:hi] for k in range(NCH)], axis=1)

    def spread_grads(lo, hi):
        for h in range(2):
            gall[lo:hi, h * C:(h + 1) * C] = lax.dot_general(
                load(lo, hi), ebuf[2 + h], (((1,), (1,)), ((), ())), preferred_element_type=F32).astype(BF16)

    def products(lo, hi):
        rows = load(lo, hi)
        for n in range(4):
            part = jnp.dot(rows, wb[:, n * 256:(n + 1) * 256], preferred_element_type=F32).astype(BF16)
            ybuf[2 * n, lo:hi] = part[:, :128]
            ybuf[2 * n + 1, lo:hi] = part[:, 128:]

    cut = GROUPS[0][1] * SLOT

    def arrived(n, sem):
        pltpu.make_async_copy(sbuf.at[pl.ds(0, n)], sbuf.at[pl.ds(0, n)], sem).wait()

    arrived(GROUPS[0][1] * NXY, x_recv0)
    products(0, cut)
    send_group(0, send_y)
    spread_grads(0, cut)

    own_x.wait()
    arrived(NCHIP - 1 - GROUPS[0][1] * NXY, x_recv1)

    spread_grads(cut, NZ * SLOT)
    theirs, ours = 4 * (1 - core), 4 * core

    def weight_grads(k):
        both = lax.dot_general(xm[k], gall[...], (((0,), (0,)), ((), ())), preferred_element_type=F32)
        gwbuf[k, 0] = both[0:CH, :C] + both[CH:2 * CH, C:]
        gwbuf[k, 1] = both[0:CH, C:] - both[CH:2 * CH, :C]

    def exchange(k):
        return pltpu.make_async_remote_copy(
            src_ref=gwbuf.at[theirs + k], dst_ref=gwx.at[k], send_sem=e_send.at[k], recv_sem=e_recv.at[k],
            device_id={"blk": blk ^ 1, "chan": c}, device_id_type=MESH)

    for k in range(4):
        weight_grads(theirs + k)
        exchange(k).start()
    for k in range(4):
        weight_grads(ours + k)
    products(cut, NZ * SLOT)
    send_slots(send_y, 3, 5, 0)
    for k in range(4):
        exchange(k).wait_recv()
        gwbuf[ours + k] += gwx[k]
        mine = ours + k == c

        @pl.when(mine)
        def _():
            pltpu.make_async_copy(gwbuf.at[ours + k], gwr.at[c & 3], d_recv).start()

        @pl.when(jnp.logical_not(mine))
        def _():
            pltpu.make_async_remote_copy(
                src_ref=gwbuf.at[ours + k], dst_ref=gwr.at[c & 3], send_sem=d_send, recv_sem=d_recv,
                device_id={"blk": j * NC + (c >> 2), "chan": ours + k}, device_id_type=MESH).start()

    send_slots(send_y, 5, 8, 0)
    own_y = pltpu.make_async_copy(ybuf.at[c, own_rows], rbuf.at[j * NCH + c], y_loc)
    own_y.start()

    def done(buf, sem):
        pltpu.make_async_copy(buf, buf, sem).wait()

    @pl.when(w_self)
    def _():
        done(wrecv.at[pl.ds(0, 3)], w_send)
        hand_over.wait_send()
        done(gwr.at[pl.ds(0, 3)], d_send)

    @pl.when(jnp.logical_not(w_self))
    def _():
        done(wrecv.at[pl.ds(0, 4)], w_send)
        done(gwr, d_send)

    arrived(NCHIP - 1, x_send)
    arrived(NCHIP - 1, y_send)
    own_y.wait()
    for k in range(4):
        exchange(k).wait_send()
    done(gwr, d_recv)
    arrived(NCHIP - 1, y_recv)


def finish(rbuf, gwr, mask_ref, out_hbm, gin_hbm, gw_hbm, b32, xf, outv, ginv, gwv, s_out, s_gin, s_gw):
    for k in range(4):
        for p in range(2):
            gwv[k, p] = gwr[k, p] * mask_ref[k:k + 1, :]
    put_gw = pltpu.make_async_copy(gwv, gw_hbm, s_gw)
    put_gw.start()

    for m in range(NCHIP):
        b32[m * PAD_M:m * PAD_M + S, :] = rbuf[m].astype(F32)
    for s in range(S):
        tile = b32[pl.ds(s, NCHIP, stride=PAD_M), :].T
        for q in range(2):
            for p in range(2):
                row = (2 * q + p) * CH
                xf[pl.ds(q * CH * PAD_O + p * S + s, CH, stride=PAD_O), :] = tile[row:row + CH]
    for q, buf in enumerate((outv, ginv)):
        for o in range(CH):
            row = (q * CH + o) * PAD_O
            buf[o] = xf[row:row + 2 * S, :].astype(BF16).reshape(2, S, 128)
        if q == 0:
            put_out = pltpu.make_async_copy(outv, out_hbm, s_out)
            put_out.start()
    put_gin = pltpu.make_async_copy(ginv, gin_hbm, s_gin)
    put_gin.start()
    put_gw.wait()
    put_out.wait()
    put_gin.wait()


def local(spec_in, weight, pattern, cotangent):
    vmem = pl.BlockSpec(memory_space=pltpu.VMEM)
    hbm = pl.BlockSpec(memory_space=pltpu.HBM)
    dma = pltpu.SemaphoreType.DMA
    tiles, sums, mask = pl.pallas_call(
        kernel,
        out_shape=(
            jax.ShapeDtypeStruct((NCHIP, S, 128), BF16),
            jax.ShapeDtypeStruct(weight.shape, F32),
            jax.ShapeDtypeStruct((4, C), F32),
        ),
        in_specs=[hbm, hbm, hbm, hbm],
        out_specs=(vmem, vmem, vmem),
        scratch_shapes=[
            pltpu.VMEM(spec_in.shape, BF16),
            pltpu.VMEM(spec_in.shape, BF16),
            pltpu.VMEM(weight.shape, BF16),
            pltpu.SMEM(pattern.shape, jnp.int32),
            pltpu.VMEM((2048, 128), F32),
            pltpu.VMEM((2048, 128), F32),
            pltpu.VMEM((NCHIP, S, 128), BF16),
            pltpu.VMEM((NCH, NZ * SLOT, 128), BF16),
            pltpu.VMEM((4, 2, CH, C), BF16),
            pltpu.VMEM((NCH, 2, CH, C), BF16),
            pltpu.VMEM((NCH * 128, NCH * 128), BF16),
            pltpu.VMEM((4, C, NCH * 128), BF16),
            pltpu.VMEM((NCH, NZ * SLOT, 128), BF16),
            pltpu.VMEM((NZ * SLOT, 2 * C), BF16),
            pltpu.VMEM((NCH, 2, CH, C), F32),
            pltpu.VMEM(weight.shape, F32),
            pltpu.SemaphoreType.REGULAR,
        ] + [dma] * 15 + [pltpu.SemaphoreType.DMA((4,))] * 2 + [dma] * 2,
        compiler_params=pltpu.CompilerParams(
            collective_id=0, has_side_effects=True, vmem_limit_bytes=40 << 20),
    )(*(pltpu.with_memory_space_constraint(a, pltpu.HBM) for a in (spec_in, weight, pattern, cotangent)))
    return pl.pallas_call(
        finish,
        out_shape=(
            jax.ShapeDtypeStruct(spec_in.shape, BF16),
            jax.ShapeDtypeStruct(spec_in.shape, BF16),
            jax.ShapeDtypeStruct(weight.shape, F32),
        ),
        in_specs=[vmem, vmem, vmem],
        out_specs=(hbm, hbm, hbm),
        scratch_shapes=[
            pltpu.VMEM((NCHIP * PAD_M, 128), F32),
            pltpu.VMEM((2 * CH * PAD_O, 128), F32),
            pltpu.VMEM(spec_in.shape, BF16),
            pltpu.VMEM(spec_in.shape, BF16),
            pltpu.VMEM(weight.shape, F32),
        ] + [dma] * 3,
        compiler_params=pltpu.CompilerParams(vmem_limit_bytes=16 << 20),
    )(tiles, sums, mask)


def solution(mesh):
    in_specs = (
        P("chan", None, "blk", None),
        P("blk", None, "chan", None),
        P("blk", None, None),
        P("chan", None, "blk", None),
    )
    out_specs = (
        P("chan", None, "blk", None),
        P("chan", None, "blk", None),
        P("blk", None, "chan", None),
    )
    return jax.shard_map(local, mesh=mesh, in_specs=in_specs, out_specs=out_specs, check_vma=False)
```
